32 devices in a mesh: group: 2 (over x), date: 16 (over z, y, core).
Axes of the slice: x: 2, y: 2, z: 4, core: 2. Of those that a mesh axis runs over, the one named last changes fastest.
Arguments:
- salvo_records: bfloat16 [32, 3, 2, 13, 1024], P(('group', 'date')), parts along dimension 0, may hold values from -6 to 6
- stencil_weights: bfloat16 [32, 3, 8], P(('group', 'date')), parts along dimension 0, may hold values from -2 to 2
- zone_drifts: int32 [32, 3], P(('group', 'date')), parts along dimension 0, may hold values from -16 to 16
- seam_sweeps: int32 [32, 2], P(('group', 'date')), parts along dimension 0, may hold values from 1 to 2
- prior_sweeps: int32 [32], P(('group', 'date')), parts along dimension 0, may hold values from 0 to 1
- viewing_frames: int32 [512, 128], P(('group', 'date')), parts along dimension 0, may hold values from 0 to 4095, as said below
Outputs:
- filtered: bfloat16 [32, 2, 32, 1024], P(('group', 'date')), parts along dimension 0
The draws below stay inside these ranges and needn't reach their ends.
There are 2 independent parts, one for each index of `group`. The reference program is written for one: setup_inputs(seed, part) draws one part's arguments, and reference() takes and returns one part's arrays. A program takes and returns all parts, laid end to end along the dimension named above; each array names one. Nothing has to cross between parts.
Inputs may be any that keep to these rules, and one draw needn't show every extreme that they name: `viewing_frames`: window w belongs to ground block g = w // 16 and names pixels line-major among 4 lines of 1024 cells: local line 0 is the line above the block, lines 1 .. 2 the block, line 3 the line below. The first block never names local line 0, the last block never names local line 3.
All inputs are finite; a program needn't handle non-finite values.
Results may differ from the reference program's by a relative error of at most 0.019.
Values may be sent and summed in bfloat16 or wider, within the bound.
No kernel may reach another device: no remote copies, remote signals or barrier semaphores. Data moves between devices by JAX's collectives and lax.ppermute only.
A program may use at most 64 MiB of HBM per device.

```python
import math
import jax
import jax.numpy as jnp
from jax import lax

LB = 2
DISTANCE_BINS = 1024
SALVO_TALLY = 3
STENCIL_WEIGHTS = 8
BAND_DRIFT_LIMIT = 16
LOOKS = 128
ITERS = 8
PATCH = 32
CAPTURE_TALLY = 16
FLIGHT_SWEEPS = 32
JOINT_SWEEPS_TOP = 2
JOINT_SWEEPS_LOW = 1
OFF = 1
SALVO_SWEEPS = 13
WIN_DEV = 16
WINDOWS = 256
N_DATE = 16


def draw_viewing_frames(key, part):
    extent = (LB + 2) * DISTANCE_BINS
    chosen = jax.random.randint(key, (WINDOWS, LOOKS), 0, extent).astype(jnp.int32)
    block_of = (jnp.arange(WINDOWS, dtype=jnp.int32) // WIN_DEV)[:, None]
    line_of = chosen // DISTANCE_BINS
    last_block = WINDOWS // WIN_DEV - 1
    chosen = jnp.where((block_of == 0) & (line_of == 0), chosen + DISTANCE_BINS, chosen)
    chosen = jnp.where((block_of == last_block) & (line_of == LB + 1), chosen - DISTANCE_BINS, chosen)
    chosen = chosen.at[0, 0].set(extent - 1)
    chosen = chosen.at[WIN_DEV, 0].set(0)
    return chosen.astype(jnp.int32)


def touch_ends(values, rng, smallest, largest):
    shape = values.shape
    place = [jax.random.randint(jax.random.fold_in(rng, axis), (), 0, shape[axis]) for axis in range(len(shape))]
    values = values.at[tuple(place)].set(smallest)
    longest = shape.index(max(shape))
    place[longest] = (place[longest] + 1) % shape[longest]
    return values.at[tuple(place)].set(largest)


def level_of(key, dims, split, least, largest):
    level, own = 1.0, jax.random.fold_in(key, 6)
    for dim, shards_of in split:
        steps = jnp.exp(jax.random.uniform(jax.random.fold_in(own, dim), (shards_of,), jnp.float32, least / len(split), largest / len(split)))
        level = level * jnp.repeat(steps, dims[dim] // shards_of).reshape([-1 if axis == dim else 1 for axis in range(len(dims))])
    return level


def centred(own_key, shape, deviation, bound, pieces=(), kind=jnp.bfloat16):
    entries = deviation * jax.random.normal(own_key, shape, jnp.float32)
    if pieces:
        entries = entries * level_of(own_key, shape, pieces, -0.22, 0.18)
    return jnp.clip(entries, -bound, bound).astype(kind)


def setup_inputs(seed: int = 0, part: int = 0) -> dict:
    seeds = jax.random.split(jax.random.key(seed), 7)
    part_splits = jax.random.split(jax.random.fold_in(seeds[6], part), 7)
    salvo_records = centred(part_splits[0], (CAPTURE_TALLY, SALVO_TALLY, 2, SALVO_SWEEPS, DISTANCE_BINS), 1.0, 6.0, ((0, 16),))
    stencil_weights = centred(part_splits[1], (CAPTURE_TALLY, SALVO_TALLY, STENCIL_WEIGHTS), STENCIL_WEIGHTS ** -0.5, 2.0, ((0, 16),))
    zone_drifts = touch_ends(jax.random.randint(part_splits[2], (CAPTURE_TALLY, SALVO_TALLY), 0 - BAND_DRIFT_LIMIT, BAND_DRIFT_LIMIT + 1), jax.random.fold_in(part_splits[2], 1), 0 - BAND_DRIFT_LIMIT, BAND_DRIFT_LIMIT).astype(jnp.int32)
    seam_sweeps = touch_ends(jax.random.randint(part_splits[3], (CAPTURE_TALLY, SALVO_TALLY - 1), JOINT_SWEEPS_LOW, JOINT_SWEEPS_TOP + 1), jax.random.fold_in(part_splits[3], 1), JOINT_SWEEPS_LOW, JOINT_SWEEPS_TOP).astype(jnp.int32)
    prior_sweeps = touch_ends(jax.random.randint(part_splits[4], (CAPTURE_TALLY,), 0, OFF + 1), jax.random.fold_in(part_splits[4], 1), 0, OFF).astype(jnp.int32)
    viewing_frames = draw_viewing_frames(jax.random.fold_in(jax.random.fold_in(seeds[6], part), 71), part)
    return {"salvo_records": salvo_records, "stencil_weights": stencil_weights, "zone_drifts": zone_drifts, "seam_sweeps": seam_sweeps, "prior_sweeps": prior_sweeps, "viewing_frames": viewing_frames}


EPSILON = 1e-06
SHRINK = 0.05

def regridding_tableau(tap_row, offset, distance_readings):
    rows = lax.broadcasted_iota(jnp.int32, (distance_readings, distance_readings), 0)
    downward_entry_list = lax.broadcasted_iota(jnp.int32, (distance_readings, distance_readings), 1)
    distance = rows - downward_entry_list - offset.astype(jnp.int32) + (STENCIL_WEIGHTS // 2 - 1)
    matrix = jnp.zeros((distance_readings, distance_readings), jnp.bfloat16)
    for tap_index in range(STENCIL_WEIGHTS):
        matrix = jnp.where(distance == tap_index, tap_row[tap_index], matrix)
    return matrix

def seam_lone_capture(piled_salvos, stencil_weight_table, distance_drifts, joint_sweep, opening_salvo, sweep_labels):
    distance_readings = piled_salvos.shape[-1]
    sweeps_each_salvo = piled_salvos.shape[2]
    regridding_zones = jnp.stack([regridding_tableau(stencil_weight_table[salvo_label], distance_drifts[salvo_label], distance_readings) for salvo_label in range(SALVO_TALLY)])
    regridded_salvos = jnp.einsum('bndo,bot->bndt', piled_salvos.astype(jnp.float32), regridding_zones.astype(jnp.float32)).astype(jnp.bfloat16)
    sweep_spacing = (sweeps_each_salvo - joint_sweep).astype(jnp.int32)
    salvo_beginnings = jnp.concatenate([jnp.zeros((1,), jnp.int32), jnp.cumsum(sweep_spacing).astype(jnp.int32)]) - opening_salvo.astype(jnp.int32)
    flight_sweep_slot = lax.broadcasted_iota(jnp.int32, (sweep_labels, sweeps_each_salvo), 0)
    sweep_slot = lax.broadcasted_iota(jnp.int32, (sweep_labels, sweeps_each_salvo), 1)
    downward_entry_list = []
    for salvo_label in range(SALVO_TALLY):
        seam_ramp = jnp.ones((sweep_labels, sweeps_each_salvo), jnp.float32)
        if salvo_label > 0:
            upward_ramp = (flight_sweep_slot - salvo_beginnings[salvo_label] + 1).astype(jnp.float32) / (joint_sweep[salvo_label - 1] + 1).astype(jnp.float32)
            seam_ramp = seam_ramp * jnp.clip(upward_ramp, 0.0, 1.0)
        if salvo_label < SALVO_TALLY - 1:
            downward_ramp = (salvo_beginnings[salvo_label] + sweeps_each_salvo - flight_sweep_slot).astype(jnp.float32) / (joint_sweep[salvo_label] + 1).astype(jnp.float32)
            seam_ramp = seam_ramp * jnp.clip(downward_ramp, 0.0, 1.0)
        downward_entry_list.append(jnp.where(flight_sweep_slot == salvo_beginnings[salvo_label] + sweep_slot, seam_ramp, 0.0).astype(jnp.bfloat16))
    sweep_target_slot = jnp.stack(downward_entry_list, axis=1)
    return jnp.einsum('tzg,zugi->uti', sweep_target_slot.astype(jnp.float32), regridded_salvos.astype(jnp.float32)).astype(jnp.bfloat16)

def coupling_frames(readings, native_picture_elements):
    sample_real = readings[:, 0].astype(jnp.float32)
    sample_imaginary = readings[:, 1].astype(jnp.float32)

    def pair(left, right):
        return jnp.einsum('dwm,ewm->wde', left, right)
    inverse_looks = 1.0 / LOOKS
    covariance_real = (pair(sample_real, sample_real) + pair(sample_imaginary, sample_imaginary)) * inverse_looks
    mixed = pair(sample_imaginary, sample_real)
    covariance_imaginary = (mixed - jnp.swapaxes(mixed, 1, 2)) * inverse_looks
    dates = readings.shape[0]
    inverse_root = lax.rsqrt(jnp.diagonal(covariance_real, axis1=1, axis2=2) + EPSILON)
    outer = inverse_root[:, :, None] * inverse_root[:, None, :]
    identity = jnp.eye(dates, dtype=jnp.float32)
    coherence_real = (1.0 - SHRINK) * covariance_real * outer + SHRINK * identity
    coherence_imaginary = (1.0 - SHRINK) * covariance_imaginary * outer
    vector_real = jnp.ones(inverse_root.shape, jnp.float32)
    vector_imaginary = jnp.zeros(inverse_root.shape, jnp.float32)

    def apply_matrix(matrix, vector):
        return jnp.einsum('wde,we->wd', matrix, vector, precision=lax.Precision.HIGHEST)
    for iteration in range(ITERS):
        image_real = apply_matrix(coherence_real, vector_real) - apply_matrix(coherence_imaginary, vector_imaginary)
        image_imaginary = apply_matrix(coherence_real, vector_imaginary) + apply_matrix(coherence_imaginary, vector_real)
        factor = lax.rsqrt(lax.optimization_barrier(jnp.mean(image_real * image_real + image_imaginary * image_imaginary, axis=1, keepdims=True)) + EPSILON)
        vector_real = image_real * factor
        vector_imaginary = image_imaginary * factor
    coupled_result = jnp.stack([vector_real, vector_imaginary]).astype(jnp.bfloat16)
    own_real = native_picture_elements[:, 0].astype(jnp.float32)
    own_imaginary = native_picture_elements[:, 1].astype(jnp.float32)
    history_real = coupled_result[0].astype(jnp.float32)
    history_imaginary = coupled_result[1].astype(jnp.float32)

    def project(history, pixels):
        return jnp.einsum('wd,dwm->wm', history, pixels)
    scaling = 1.0 / math.sqrt(dates)
    compressed_real = (project(history_real, own_real) + project(history_imaginary, own_imaginary)) * scaling
    compressed_imaginary = (project(history_real, own_imaginary) - project(history_imaginary, own_real)) * scaling
    condensed_result = jnp.stack([compressed_real, compressed_imaginary]).astype(jnp.bfloat16)
    return (condensed_result, coupled_result)

def dft_tables(length, span):
    first = lax.broadcasted_iota(jnp.int32, (span, span), 0)
    second = lax.broadcasted_iota(jnp.int32, (span, span), 1)
    product = first % length * (second % length) % length
    angle = product.astype(jnp.float32) * (2.0 * math.pi / length)
    inside = first // length == second // length
    cosine = jnp.where(inside, jnp.cos(angle), 0.0).astype(jnp.bfloat16)
    sine = jnp.where(inside, jnp.sin(angle), 0.0).astype(jnp.bfloat16)
    return (cosine, sine)

def goldstein(rebuilt):
    sweep_labels = rebuilt.shape[1]
    distance_readings = rebuilt.shape[2]
    range_cos, range_sin = dft_tables(PATCH, 128)
    line_cos, line_sin = dft_tables(PATCH, PATCH)

    def across(matrix, table):
        return jnp.dot(matrix.reshape(-1, 128), table, preferred_element_type=jnp.float32).reshape(sweep_labels, distance_readings)

    def along(table, matrix):
        return jnp.einsum('kn,pnr->pkr', table.astype(jnp.float32), matrix.reshape(sweep_labels // PATCH, PATCH, distance_readings).astype(jnp.float32))
    real_in = rebuilt[0]
    imaginary_in = rebuilt[1]
    first_real = (across(real_in, range_cos) + across(imaginary_in, range_sin)).astype(jnp.bfloat16)
    first_imaginary = (across(imaginary_in, range_cos) - across(real_in, range_sin)).astype(jnp.bfloat16)
    spectrum_real = along(line_cos, first_real) + along(line_sin, first_imaginary)
    spectrum_imaginary = along(line_cos, first_imaginary) - along(line_sin, first_real)
    power = spectrum_real * spectrum_real + spectrum_imaginary * spectrum_imaginary
    patch_total = lax.optimization_barrier(jnp.sum(power, axis=1)).reshape(sweep_labels // PATCH, distance_readings // PATCH, PATCH).sum(axis=2)
    patch_mean = jnp.repeat(patch_total / (PATCH * PATCH), PATCH, axis=1)[:, None, :]
    seam_ramp = jnp.sqrt(jnp.sqrt(power / (patch_mean + EPSILON)))
    weighted_real = (spectrum_real * seam_ramp).astype(jnp.bfloat16)
    weighted_imaginary = (spectrum_imaginary * seam_ramp).astype(jnp.bfloat16)
    back_real = (along(line_cos, weighted_real) - along(line_sin, weighted_imaginary)).astype(jnp.bfloat16)
    back_imaginary = (along(line_cos, weighted_imaginary) + along(line_sin, weighted_real)).astype(jnp.bfloat16)
    scaling = 1.0 / (PATCH * PATCH)
    out_real = ((across(back_real, range_cos) - across(back_imaginary, range_sin)) * scaling).astype(jnp.bfloat16)
    out_imaginary = ((across(back_imaginary, range_cos) + across(back_real, range_sin)) * scaling).astype(jnp.bfloat16)
    return jnp.stack([out_real, out_imaginary])

def reference(salvo_records, stencil_weights, zone_drifts, seam_sweeps, prior_sweeps, viewing_frames):
    seamed_picture = lax.map(lambda salvo_components: seam_lone_capture(salvo_components[0], salvo_components[1], salvo_components[2], salvo_components[3], salvo_components[4], FLIGHT_SWEEPS), (salvo_records, stencil_weights, zone_drifts, seam_sweeps, prior_sweeps))
    padded = jnp.pad(seamed_picture, ((0, 0), (0, 0), (1, 1), (0, 0)))
    flat = padded.reshape(CAPTURE_TALLY, 2, (FLIGHT_SWEEPS + 2) * DISTANCE_BINS)
    window_index = lax.broadcasted_iota(jnp.int32, (WINDOWS, LOOKS), 0)
    global_index = (window_index // WIN_DEV * (LB * DISTANCE_BINS) + viewing_frames.astype(jnp.int32)).astype(jnp.int32)
    readings = jnp.take(flat, global_index.reshape(-1), axis=2).reshape(CAPTURE_TALLY, 2, N_DATE, WIN_DEV, LOOKS)
    native_picture_elements = seamed_picture.reshape(CAPTURE_TALLY, 2, N_DATE, WIN_DEV, LOOKS)
    readings = jnp.moveaxis(readings, 2, 0)
    native_picture_elements = jnp.moveaxis(native_picture_elements, 2, 0)
    condensed_result, coupled_result = lax.map(lambda salvo_components: coupling_frames(salvo_components[0], salvo_components[1]), (readings, native_picture_elements))
    condensed_result = jnp.moveaxis(condensed_result, 0, 1).reshape(2, WINDOWS, LOOKS)
    coupled_result = jnp.moveaxis(coupled_result, 0, 1).reshape(2, WINDOWS, CAPTURE_TALLY)
    value_real = condensed_result[0].astype(jnp.float32)
    value_imaginary = condensed_result[1].astype(jnp.float32)

    def per_date(history):
        history_real = history[0].astype(jnp.float32)[:, None]
        history_imaginary = history[1].astype(jnp.float32)[:, None]
        rebuilt = jnp.stack([value_real * history_real - value_imaginary * history_imaginary, value_real * history_imaginary + value_imaginary * history_real]).astype(jnp.bfloat16)
        return goldstein(rebuilt.reshape(2, FLIGHT_SWEEPS, DISTANCE_BINS))
    return lax.map(per_date, jnp.transpose(coupled_result, (2, 0, 1)))
```

```python
import functools
import math

import jax
import jax.numpy as jnp
import numpy as np
from jax import lax
from jax.experimental import pallas as pl
from jax.experimental.pallas import tpu as pltpu
from jax.sharding import PartitionSpec as P

LB = 2
SALVO_TALLY = 3
STENCIL_WEIGHTS = 8
LOOKS = 128
ITERS = 8
PATCH = 32
LANES = 128

EPSILON = 1e-06
SHRINK = 0.05

HALO = LB + 2
F32 = jnp.float32
BF16 = jnp.bfloat16
NT = (((1,), (1,)), ((), ()))


def iota(shape, axis):
    return lax.broadcasted_iota(jnp.int32, shape, axis)


def seam_kernel(drifts, seams, prior, weights, bursts, out, held, *, sweep_labels):
    sweeps, cells = bursts.shape[3:]
    slot = held.shape[0] // (2 * SALVO_TALLY)
    span = cells + LANES
    held[...] = jnp.zeros(held.shape, held.dtype)
    taps = weights[0].astype(F32)
    for b in range(SALVO_TALLY):
        first = span + (STENCIL_WEIGHTS // 2 - 1) - drifts[0, b]
        first = jnp.where(first >= span, first - span, first)
        for c in range(2):
            row = jnp.concatenate(
                [bursts[0, b, c].astype(F32), jnp.zeros((sweeps, LANES), F32)], axis=1
            )
            row = pltpu.roll(row, first, 1)
            total = row * taps[b : b + 1, 0:1]
            for k in range(1, STENCIL_WEIGHTS):
                total = total + pltpu.roll(row, span - k, 1) * taps[b : b + 1, k : k + 1]
            base = (c * SALVO_TALLY + b) * slot
            held[base : base + sweeps, :] = total[:, :cells].astype(BF16)
    shape = (out.shape[0] * 2 * HALO, held.shape[0])
    bits = slot.bit_length() - 1
    row, column = iota(shape, 0), iota(shape, 1)
    line = (row // (2 * HALO)) * LB - 1 + row % HALO
    part = (row // HALO) % 2
    which = lax.shift_right_logical(column, bits)
    entry = column & (slot - 1)
    place = jnp.zeros(shape, F32)
    start = -prior[0]
    for b in range(SALVO_TALLY):
        ramp = jnp.ones(shape, F32)
        if b > 0:
            start = start + sweeps - seams[0, b - 1]
            up = (line - start + 1).astype(F32) / (seams[0, b - 1] + 1).astype(F32)
            ramp = ramp * jnp.clip(up, 0.0, 1.0)
        if b < SALVO_TALLY - 1:
            down = (start + sweeps - line).astype(F32) / (seams[0, b] + 1).astype(F32)
            ramp = ramp * jnp.clip(down, 0.0, 1.0)
        here = (which == part * SALVO_TALLY + b) & (line == start + entry)
        place = jnp.where(here, ramp, place)
    inside = (entry < sweeps) & (line >= 0) & (line < sweep_labels)
    place = jnp.where(inside, place, 0.0).astype(BF16)
    merged = jnp.dot(place, held[...], preferred_element_type=F32)
    out[...] = merged.reshape(out.shape).astype(BF16)


def seam(bursts, weights, drifts, seams, prior, devices):
    sweeps, cells = bursts.shape[3:]
    slot = 16
    while slot < sweeps:
        slot *= 2
    smem = pl.BlockSpec(memory_space=pltpu.SMEM)
    vmem = pl.BlockSpec(memory_space=pltpu.VMEM)
    return pl.pallas_call(
        functools.partial(seam_kernel, sweep_labels=LB * devices),
        out_shape=jax.ShapeDtypeStruct((devices, 2 * HALO, cells), BF16),
        in_specs=[smem, smem, smem, vmem, vmem],
        out_specs=vmem,
        scratch_shapes=[pltpu.VMEM((2 * SALVO_TALLY * slot, cells), BF16)],
    )(drifts, seams, prior, weights, bursts)


def link_kernel(frames, ground, out, wide, table, left, right32, rebuilt):
    dates, _, cells = ground.shape
    windows = frames.shape[0]
    depth = 2 * dates
    span = depth * windows
    chunks = cells // LANES
    rows = ground[...].astype(F32).reshape(dates * 2 * HALO, cells)
    for j in range(chunks):
        wide[j] = rows[:, j * LANES : (j + 1) * LANES]
        for r in range(2 * HALO):
            table[r, j] = wide[j, pl.ds(r, dates, stride=2 * HALO), :]

    def collect(w, carry):
        pixel = frames[pl.ds(w, 1), :]
        low = jnp.broadcast_to(pixel & (LANES - 1), (8, LANES))
        high = jnp.broadcast_to(lax.shift_right_logical(pixel, 7), (8, LANES))
        found = [[jnp.zeros((8, LANES), F32) for _ in range(dates // 8)] for _ in range(2)]
        for t in range(HALO):
            for j in range(chunks):
                here = high == t * chunks + j
                for c in range(2):
                    for g in range(dates // 8):
                        tile = table[c * HALO + t, j, g * 8 : g * 8 + 8, :]
                        taken = jnp.take_along_axis(tile, low, axis=1, mode="promise_in_bounds")
                        found[c][g] = jnp.where(here, taken, found[c][g])
        real = jnp.concatenate(found[0], axis=0)
        imaginary = jnp.concatenate(found[1], axis=0)
        pieces = ((real, 0, 0), (imaginary, 1, 0), (-imaginary, 0, 1), (real, 1, 1))
        for value, c, half in pieces:
            left[w, c * dates : (c + 1) * dates, pl.ds(half * LANES, LANES)] = value.astype(BF16)
            right32[half, pl.ds(c * dates * windows + w, dates, stride=windows), :] = value
        return carry

    lax.fori_loop(0, windows, collect, 0)
    products = lax.dot_general(
        left[...].reshape(span, 2 * LANES),
        jnp.concatenate([right32[0], right32[1]], axis=1).astype(BF16),
        NT,
        preferred_element_type=F32,
    )
    owner = iota((depth, span), 1) & (windows - 1)
    cov = jnp.zeros((depth, span), F32)
    for w in range(windows):
        cov = jnp.where(owner == w, products[w * depth : (w + 1) * depth], cov)
    cov = cov * (1.0 / LOOKS)

    def over_lanes(value):
        total = value[:, :LANES]
        for j in range(1, span // LANES):
            total = total + value[:, j * LANES : (j + 1) * LANES]
        shift = windows
        while shift < LANES:
            total = total + pltpu.roll(total, shift, 1)
            shift *= 2
        return total

    def over_rows(value):
        return jnp.sum(value, axis=0, keepdims=True)

    def spread(value):
        return jnp.concatenate([value] * (span // LANES), axis=1)

    bits = windows.bit_length() - 1
    same = lax.shift_right_logical(iota((depth, span), 1), bits) == iota((depth, span), 0)
    diagonal = jnp.where(same, cov, 0.0)
    by_lane = lax.rsqrt(over_rows(diagonal) + EPSILON)
    by_row = lax.rsqrt(over_lanes(diagonal) + EPSILON)
    gam = (1.0 - SHRINK) * cov * spread(by_row) * by_lane + jnp.where(same, SHRINK, 0.0)

    y = jnp.where(iota((depth, LANES), 0) < dates, 1.0, 0.0)
    scale = jnp.ones((1, LANES), F32)
    for step in range(ITERS // 2):
        line = over_rows(gam * spread(y))
        size = over_lanes(line * line) * (1.0 / dates)
        scale = scale * lax.rsqrt(scale * scale * size + EPSILON)
        y = over_lanes(gam * line)
        size = over_rows(y * y) * (1.0 / dates)
        scale = scale * lax.rsqrt(scale * scale * size + EPSILON)
    linked = (y * scale).astype(BF16).astype(F32)

    factor = 1.0 / math.sqrt(dates)
    for w in range(windows):
        t, at = (w * LOOKS) // cells, (w * LOOKS) % cells
        column = jnp.broadcast_to(linked[:, w : w + 1], (depth, LANES))
        real, imaginary = column[:dates], column[dates:]
        own_real = table[1 + t, at // LANES]
        own_imaginary = table[HALO + 1 + t, at // LANES]
        value_real = over_rows(real * own_real + imaginary * own_imaginary) * factor
        value_imaginary = over_rows(real * own_imaginary - imaginary * own_real) * factor
        value_real = value_real.astype(BF16).astype(F32)
        value_imaginary = value_imaginary.astype(BF16).astype(F32)
        rebuilt[at // LANES, pl.ds(t, dates, stride=2 * LB), :] = (
            value_real * real - value_imaginary * imaginary
        )
        rebuilt[at // LANES, pl.ds(LB + t, dates, stride=2 * LB), :] = (
            value_real * imaginary + value_imaginary * real
        )
    for d in range(dates):
        for j in range(chunks):
            out[d, :, j * LANES : (j + 1) * LANES] = rebuilt[
                j, d * 2 * LB : (d + 1) * 2 * LB, :
            ].astype(BF16)


def link(ground, frames):
    dates, _, cells = ground.shape
    windows = frames.shape[0]
    depth = 2 * dates
    vmem = pl.BlockSpec(memory_space=pltpu.VMEM)
    return pl.pallas_call(
        link_kernel,
        out_shape=jax.ShapeDtypeStruct((dates, 2 * LB, cells), BF16),
        in_specs=[vmem, vmem],
        out_specs=vmem,
        scratch_shapes=[
            pltpu.VMEM((cells // LANES, dates * 2 * HALO, LANES), F32),
            pltpu.VMEM((2 * HALO, cells // LANES, dates, LANES), F32),
            pltpu.VMEM((windows, depth, 2 * LANES), BF16),
            pltpu.VMEM((2, depth * windows, LANES), F32),
            pltpu.VMEM((cells // LANES, dates * 2 * LB, LANES), F32),
        ],
    )(frames, ground)


def coupling_frames(readings, native_picture_elements):
    sample_real = readings[:, 0]
    sample_imaginary = readings[:, 1]

    def pair(left, right):
        return jnp.einsum("dwm,ewm->wde", left, right, preferred_element_type=F32)

    inverse_looks = 1.0 / LOOKS
    covariance_real = (
        pair(sample_real, sample_real) + pair(sample_imaginary, sample_imaginary)
    ) * inverse_looks
    mixed = pair(sample_imaginary, sample_real)
    covariance_imaginary = (mixed - jnp.swapaxes(mixed, 1, 2)) * inverse_looks
    dates = readings.shape[0]
    inverse_root = lax.rsqrt(jnp.diagonal(covariance_real, axis1=1, axis2=2) + EPSILON)
    outer = inverse_root[:, :, None] * inverse_root[:, None, :]
    identity = jnp.eye(dates, dtype=F32)
    coherence_real = (1.0 - SHRINK) * covariance_real * outer + SHRINK * identity
    coherence_imaginary = (1.0 - SHRINK) * covariance_imaginary * outer
    vector_real = jnp.ones(inverse_root.shape, F32)
    vector_imaginary = jnp.zeros(inverse_root.shape, F32)

    def apply_matrix(matrix, vector):
        return jnp.einsum("wde,we->wd", matrix, vector, precision=lax.Precision.HIGHEST)

    for iteration in range(ITERS):
        image_real = apply_matrix(coherence_real, vector_real) - apply_matrix(
            coherence_imaginary, vector_imaginary
        )
        image_imaginary = apply_matrix(coherence_real, vector_imaginary) + apply_matrix(
            coherence_imaginary, vector_real
        )
        power = image_real * image_real + image_imaginary * image_imaginary
        factor = lax.rsqrt(jnp.mean(power, axis=1, keepdims=True) + EPSILON)
        vector_real = image_real * factor
        vector_imaginary = image_imaginary * factor
    coupled_result = jnp.stack([vector_real, vector_imaginary]).astype(BF16)

    def project(history, pixels):
        return jnp.einsum("wd,dwm->wm", history, pixels, preferred_element_type=F32)

    scaling = 1.0 / math.sqrt(dates)
    own_real = native_picture_elements[:, 0]
    own_imaginary = native_picture_elements[:, 1]
    compressed_real = (
        project(coupled_result[0], own_real) + project(coupled_result[1], own_imaginary)
    ) * scaling
    compressed_imaginary = (
        project(coupled_result[0], own_imaginary) - project(coupled_result[1], own_real)
    ) * scaling
    condensed_result = jnp.stack([compressed_real, compressed_imaginary]).astype(BF16)
    return (condensed_result, coupled_result)


def link_plain(ground, frames):
    dates, _, cells = ground.shape
    windows = frames.shape[0]
    extended = ground.reshape(dates, 2, HALO, cells)
    flat = extended.reshape(dates, 2, HALO * cells)
    readings = jnp.take(flat, frames.reshape(-1), axis=2).reshape(dates, 2, windows, LOOKS)
    native = extended[:, :, 1 : LB + 1].reshape(dates, 2, windows, LOOKS)
    condensed_result, coupled_result = coupling_frames(readings, native)
    history_real = coupled_result[0].astype(F32).T[:, :, None]
    history_imaginary = coupled_result[1].astype(F32).T[:, :, None]
    value_real = condensed_result[0].astype(F32)[None]
    value_imaginary = condensed_result[1].astype(F32)[None]
    rebuilt = jnp.stack(
        [
            value_real * history_real - value_imaginary * history_imaginary,
            value_real * history_imaginary + value_imaginary * history_real,
        ],
        axis=1,
    ).astype(BF16)
    return rebuilt.reshape(dates, 2 * LB, cells)


def dft_tables(length, span):
    first, second = np.arange(span)[:, None], np.arange(span)[None, :]
    angle = (first % length) * (second % length) % length * (2.0 * math.pi / length)
    inside = first // length == second // length
    return np.where(inside, np.cos(angle), 0.0), np.where(inside, np.sin(angle), 0.0)


def patch_kernel(range_table, ahead_table, back_table, mine, out, wide):
    blocks, _, cells = mine.shape
    chunks = cells // LANES

    def cut(value, j):
        return value[:, j * LANES : (j + 1) * LANES]

    for b in range(blocks):
        rows = mine[b].astype(F32)
        for j in range(chunks):
            wide[j, b * 2 * LB : (b + 1) * 2 * LB, :] = cut(rows, j)

    def lines_of(c, j):
        pieces = [wide[j, pl.ds(c * LB + t, blocks, stride=2 * LB), :] for t in range(LB)]
        return jnp.concatenate(pieces, axis=0).astype(BF16)

    first = jnp.concatenate(
        [
            jnp.concatenate([lines_of(0, j), lines_of(1, j)], axis=1)
            for j in range(chunks)
        ],
        axis=0,
    )

    def by_chunk(real, imaginary):
        return jnp.concatenate(
            [
                jnp.concatenate([cut(real, j), cut(imaginary, j)], axis=1)
                for j in range(chunks)
            ],
            axis=0,
        )

    def by_line(value, c):
        return jnp.concatenate(
            [cut(value[j * PATCH : (j + 1) * PATCH], c) for j in range(chunks)], axis=1
        )

    table = range_table[...]
    across = jnp.dot(first, table, preferred_element_type=F32).astype(BF16)
    across = jnp.concatenate([by_line(across, 0), by_line(across, 1)], axis=0)
    spectrum = jnp.dot(ahead_table[...], across, preferred_element_type=F32)
    real, imaginary = spectrum[:PATCH], spectrum[PATCH:]
    power = real * real + imaginary * imaginary
    total = jnp.sum(power, axis=0, keepdims=True)
    total = jnp.concatenate([cut(total, j) for j in range(chunks)], axis=0)
    lane = iota(total.shape, 1)
    shift = 1
    while shift < PATCH:
        other = jnp.where(
            (lane & shift) == 0, pltpu.roll(total, LANES - shift, 1), pltpu.roll(total, shift, 1)
        )
        total = total + other
        shift *= 2
    mean = total * (1.0 / (PATCH * PATCH)) + EPSILON
    mean = jnp.concatenate([mean[j : j + 1] for j in range(chunks)], axis=1)
    ramp = jnp.sqrt(jnp.sqrt(power / mean))
    weighted = jnp.concatenate([real * ramp, imaginary * ramp], axis=0).astype(BF16)
    back = jnp.dot(back_table[...], weighted, preferred_element_type=F32).astype(BF16)
    back = by_chunk(back[:PATCH], back[PATCH:])
    final = lax.dot_general(back, table, NT, preferred_element_type=F32)
    final = (final * (1.0 / (PATCH * PATCH))).astype(BF16)
    for c in range(2):
        out[0, c] = by_line(final, c)


def patch_filter(mine, lines):
    cells = mine.shape[2]
    blocks = PATCH // LB
    cosine, sine = dft_tables(PATCH, LANES)
    range_table = np.block([[cosine, -sine], [sine, cosine]])
    cosine, sine = dft_tables(PATCH, PATCH)
    order = np.arange(PATCH).reshape(blocks, LB).T.reshape(-1)
    ahead = np.block([[cosine[:, order], sine[:, order]], [-sine[:, order], cosine[:, order]]])
    back = np.block([[cosine, -sine], [sine, cosine]])
    tables = [jnp.asarray(entry, F32).astype(BF16) for entry in (range_table, ahead, back)]
    return pl.pallas_call(
        patch_kernel,
        grid=(lines // PATCH,),
        out_shape=jax.ShapeDtypeStruct((1, 2, lines, cells), BF16),
        in_specs=[
            pl.BlockSpec((2 * LANES, 2 * LANES), lambda p: (0, 0)),
            pl.BlockSpec((2 * PATCH, 2 * PATCH), lambda p: (0, 0)),
            pl.BlockSpec((2 * PATCH, 2 * PATCH), lambda p: (0, 0)),
            pl.BlockSpec((blocks, 2 * LB, cells), lambda p: (p, 0, 0)),
        ],
        out_specs=pl.BlockSpec((1, 2, PATCH, cells), lambda p: (0, 0, p, 0)),
        scratch_shapes=[pltpu.VMEM((cells // LANES, blocks * 2 * LB, LANES), F32)],
    )(*tables, mine)


def on_device(
    salvo_records, stencil_weights, zone_drifts, seam_sweeps, prior_sweeps, viewing_frames
):
    devices = lax.axis_size("date")
    merged = seam(
        salvo_records, stencil_weights, zone_drifts, seam_sweeps, prior_sweeps, devices
    )
    ground = lax.all_to_all(merged, "date", split_axis=0, concat_axis=0, tiled=True)
    windows = viewing_frames.shape[0]
    fits = devices <= 32 and devices % 16 == 0 and LANES % windows == 0
    rebuilt = (link if fits else link_plain)(ground, viewing_frames)
    mine = lax.all_to_all(rebuilt, "date", split_axis=0, concat_axis=0, tiled=True)
    return patch_filter(mine, LB * devices)


def solution(mesh):
    in_specs = (
        P(("group", "date"), None, None, None, None),
        P(("group", "date"), None, None),
        P(("group", "date"), None),
        P(("group", "date"), None),
        P(("group", "date")),
        P(("group", "date"), None),
    )
    out_specs = P(("group", "date"), None, None, None)
    return jax.shard_map(
        on_device, mesh=mesh, in_specs=in_specs, out_specs=out_specs, check_vma=False
    )
```

```python
import functools
import math

import jax
import jax.numpy as jnp
import numpy as np
from jax import lax
from jax.experimental import pallas as pl
from jax.experimental.pallas import tpu as pltpu
from jax.sharding import PartitionSpec as P

LB = 2
SALVO_TALLY = 3
STENCIL_WEIGHTS = 8
LOOKS = 128
ITERS = 8
PATCH = 32
LANES = 128

EPSILON = 1e-06
SHRINK = 0.05

HALO = LB + 2
F32 = jnp.float32
BF16 = jnp.bfloat16
NT = (((1,), (1,)), ((), ()))


def iota(shape, axis):
    return lax.broadcasted_iota(jnp.int32, shape, axis)


def grant(devices):
    return pltpu.CompilerParams(vmem_limit_bytes=min(devices, 120) * 2**19)


def seam_kernel(drifts, seams, prior, weights, bursts, out, held, *, sweep_labels):
    sweeps, cells = bursts.shape[3:]
    slot = held.shape[0] // (2 * SALVO_TALLY)
    span = cells + LANES
    held[...] = jnp.zeros(held.shape, held.dtype)
    taps = weights[0].astype(F32)
    for b in range(SALVO_TALLY):
        first = span + (STENCIL_WEIGHTS // 2 - 1) - drifts[0, b]
        first = jnp.where(first >= span, first - span, first)
        for c in range(2):
            row = jnp.concatenate(
                [bursts[0, b, c].astype(F32), jnp.zeros((sweeps, LANES), F32)], axis=1
            )
            row = pltpu.roll(row, first, 1)
            total = row * taps[b : b + 1, 0:1]
            for k in range(1, STENCIL_WEIGHTS):
                total = total + pltpu.roll(row, span - k, 1) * taps[b : b + 1, k : k + 1]
            base = (c * SALVO_TALLY + b) * slot
            held[base : base + sweeps, :] = total[:, :cells].astype(BF16)
    shape = (out.shape[0] * 2 * HALO, held.shape[0])
    bits = slot.bit_length() - 1
    row, column = iota(shape, 0), iota(shape, 1)
    line = (row // (2 * HALO)) * LB - 1 + row % HALO
    part = (row // HALO) % 2
    which = lax.shift_right_logical(column, bits)
    entry = column & (slot - 1)
    place = jnp.zeros(shape, F32)
    start = -prior[0]
    for b in range(SALVO_TALLY):
        ramp = jnp.ones(shape, F32)
        if b > 0:
            start = start + sweeps - seams[0, b - 1]
            up = (line - start + 1).astype(F32) / (seams[0, b - 1] + 1).astype(F32)
            ramp = ramp * jnp.clip(up, 0.0, 1.0)
        if b < SALVO_TALLY - 1:
            down = (start + sweeps - line).astype(F32) / (seams[0, b] + 1).astype(F32)
            ramp = ramp * jnp.clip(down, 0.0, 1.0)
        here = (which == part * SALVO_TALLY + b) & (line == start + entry)
        place = jnp.where(here, ramp, place)
    inside = (entry < sweeps) & (line >= 0) & (line < sweep_labels)
    place = jnp.where(inside, place, 0.0).astype(BF16)
    merged = jnp.dot(place, held[...], preferred_element_type=F32)
    out[...] = merged.reshape(out.shape).astype(BF16)


def seam(bursts, weights, drifts, seams, prior, devices):
    sweeps, cells = bursts.shape[3:]
    slot = 16
    while slot < sweeps:
        slot *= 2
    smem = pl.BlockSpec(memory_space=pltpu.SMEM)
    vmem = pl.BlockSpec(memory_space=pltpu.VMEM)
    return pl.pallas_call(
        functools.partial(seam_kernel, sweep_labels=LB * devices),
        out_shape=jax.ShapeDtypeStruct((devices, 2 * HALO, cells), BF16),
        in_specs=[smem, smem, smem, vmem, vmem],
        out_specs=vmem,
        scratch_shapes=[pltpu.VMEM((2 * SALVO_TALLY * slot, cells), BF16)],
        compiler_params=grant(devices),
    )(drifts, seams, prior, weights, bursts)


def link_kernel(frames, ground, out, wide, table, left, right32, rebuilt):
    dates, _, cells = ground.shape
    windows = frames.shape[0]
    depth = 2 * dates
    span = depth * windows
    chunks = cells // LANES
    rows = ground[...].astype(F32).reshape(dates * 2 * HALO, cells)
    for j in range(chunks):
        wide[j] = rows[:, j * LANES : (j + 1) * LANES]
        for r in range(2 * HALO):
            table[r, j] = wide[j, pl.ds(r, dates, stride=2 * HALO), :]

    def collect(w, carry):
        pixel = frames[pl.ds(w, 1), :]
        low = jnp.broadcast_to(pixel & (LANES - 1), (8, LANES))
        high = jnp.broadcast_to(lax.shift_right_logical(pixel, 7), (8, LANES))
        found = [[jnp.zeros((8, LANES), F32) for _ in range(dates // 8)] for _ in range(2)]
        for t in range(HALO):
            for j in range(chunks):
                here = high == t * chunks + j
                for c in range(2):
                    for g in range(dates // 8):
                        tile = table[c * HALO + t, j, g * 8 : g * 8 + 8, :]
                        taken = jnp.take_along_axis(tile, low, axis=1, mode="promise_in_bounds")
                        found[c][g] = jnp.where(here, taken, found[c][g])
        real = jnp.concatenate(found[0], axis=0)
        imaginary = jnp.concatenate(found[1], axis=0)
        pieces = ((real, 0, 0), (imaginary, 1, 0), (-imaginary, 0, 1), (real, 1, 1))
        for value, c, half in pieces:
            left[w, c * dates : (c + 1) * dates, pl.ds(half * LANES, LANES)] = value.astype(BF16)
            right32[half, pl.ds(c * dates * windows + w, dates, stride=windows), :] = value
        return carry

    lax.fori_loop(0, windows, collect, 0)
    products = lax.dot_general(
        left[...].reshape(span, 2 * LANES),
        jnp.concatenate([right32[0], right32[1]], axis=1).astype(BF16),
        NT,
        preferred_element_type=F32,
    )
    owner = iota((depth, span), 1) & (windows - 1)
    cov = jnp.zeros((depth, span), F32)
    for w in range(windows):
        cov = jnp.where(owner == w, products[w * depth : (w + 1) * depth], cov)
    cov = cov * (1.0 / LOOKS)

    def over_lanes(value):
        total = value[:, :LANES]
        for j in range(1, span // LANES):
            total = total + value[:, j * LANES : (j + 1) * LANES]
        shift = windows
        while shift < LANES:
            total = total + pltpu.roll(total, shift, 1)
            shift *= 2
        return total

    def over_rows(value):
        return jnp.sum(value, axis=0, keepdims=True)

    def spread(value):
        return jnp.concatenate([value] * (span // LANES), axis=1)

    bits = windows.bit_length() - 1
    same = lax.shift_right_logical(iota((depth, span), 1), bits) == iota((depth, span), 0)
    diagonal = jnp.where(same, cov, 0.0)
    by_lane = lax.rsqrt(over_rows(diagonal) + EPSILON)
    by_row = lax.rsqrt(over_lanes(diagonal) + EPSILON)
    gam = (1.0 - SHRINK) * cov * spread(by_row) * by_lane + jnp.where(same, SHRINK, 0.0)

    y = jnp.where(iota((depth, LANES), 0) < dates, 1.0, 0.0)
    scale = jnp.ones((1, LANES), F32)
    for step in range(ITERS // 2):
        line = over_rows(gam * spread(y))
        size = over_lanes(line * line) * (1.0 / dates)
        scale = scale * lax.rsqrt(scale * scale * size + EPSILON)
        y = over_lanes(gam * line)
        size = over_rows(y * y) * (1.0 / dates)
        scale = scale * lax.rsqrt(scale * scale * size + EPSILON)
    linked = (y * scale).astype(BF16).astype(F32)

    factor = 1.0 / math.sqrt(dates)
    for w in range(windows):
        t, at = (w * LOOKS) // cells, (w * LOOKS) % cells
        column = jnp.broadcast_to(linked[:, w : w + 1], (depth, LANES))
        real, imaginary = column[:dates], column[dates:]
        own_real = table[1 + t, at // LANES]
        own_imaginary = table[HALO + 1 + t, at // LANES]
        value_real = over_rows(real * own_real + imaginary * own_imaginary) * factor
        value_imaginary = over_rows(real * own_imaginary - imaginary * own_real) * factor
        value_real = value_real.astype(BF16).astype(F32)
        value_imaginary = value_imaginary.astype(BF16).astype(F32)
        rebuilt[at // LANES, pl.ds(t, dates, stride=2 * LB), :] = (
            value_real * real - value_imaginary * imaginary
        )
        rebuilt[at // LANES, pl.ds(LB + t, dates, stride=2 * LB), :] = (
            value_real * imaginary + value_imaginary * real
        )
    for d in range(dates):
        for j in range(chunks):
            out[d, :, j * LANES : (j + 1) * LANES] = rebuilt[
                j, d * 2 * LB : (d + 1) * 2 * LB, :
            ].astype(BF16)


def link(ground, frames):
    dates, _, cells = ground.shape
    windows = frames.shape[0]
    depth = 2 * dates
    vmem = pl.BlockSpec(memory_space=pltpu.VMEM)
    return pl.pallas_call(
        link_kernel,
        out_shape=jax.ShapeDtypeStruct((dates, 2 * LB, cells), BF16),
        in_specs=[vmem, vmem],
        out_specs=vmem,
        scratch_shapes=[
            pltpu.VMEM((cells // LANES, dates * 2 * HALO, LANES), F32),
            pltpu.VMEM((2 * HALO, cells // LANES, dates, LANES), F32),
            pltpu.VMEM((windows, depth, 2 * LANES), BF16),
            pltpu.VMEM((2, depth * windows, LANES), F32),
            pltpu.VMEM((cells // LANES, dates * 2 * LB, LANES), F32),
        ],
        compiler_params=grant(dates),
    )(frames, ground)


def coupling_frames(readings, native_picture_elements):
    sample_real = readings[:, 0]
    sample_imaginary = readings[:, 1]

    def pair(left, right):
        return jnp.einsum("dwm,ewm->wde", left, right, preferred_element_type=F32)

    inverse_looks = 1.0 / LOOKS
    covariance_real = (
        pair(sample_real, sample_real) + pair(sample_imaginary, sample_imaginary)
    ) * inverse_looks
    mixed = pair(sample_imaginary, sample_real)
    covariance_imaginary = (mixed - jnp.swapaxes(mixed, 1, 2)) * inverse_looks
    dates = readings.shape[0]
    inverse_root = lax.rsqrt(jnp.diagonal(covariance_real, axis1=1, axis2=2) + EPSILON)
    outer = inverse_root[:, :, None] * inverse_root[:, None, :]
    identity = jnp.eye(dates, dtype=F32)
    coherence_real = (1.0 - SHRINK) * covariance_real * outer + SHRINK * identity
    coherence_imaginary = (1.0 - SHRINK) * covariance_imaginary * outer
    vector_real = jnp.ones(inverse_root.shape, F32)
    vector_imaginary = jnp.zeros(inverse_root.shape, F32)

    def apply_matrix(matrix, vector):
        return jnp.einsum("wde,we->wd", matrix, vector, precision=lax.Precision.HIGHEST)

    for iteration in range(ITERS):
        image_real = apply_matrix(coherence_real, vector_real) - apply_matrix(
            coherence_imaginary, vector_imaginary
        )
        image_imaginary = apply_matrix(coherence_real, vector_imaginary) + apply_matrix(
            coherence_imaginary, vector_real
        )
        power = image_real * image_real + image_imaginary * image_imaginary
        factor = lax.rsqrt(jnp.mean(power, axis=1, keepdims=True) + EPSILON)
        vector_real = image_real * factor
        vector_imaginary = image_imaginary * factor
    coupled_result = jnp.stack([vector_real, vector_imaginary]).astype(BF16)

    def project(history, pixels):
        return jnp.einsum("wd,dwm->wm", history, pixels, preferred_element_type=F32)

    scaling = 1.0 / math.sqrt(dates)
    own_real = native_picture_elements[:, 0]
    own_imaginary = native_picture_elements[:, 1]
    compressed_real = (
        project(coupled_result[0], own_real) + project(coupled_result[1], own_imaginary)
    ) * scaling
    compressed_imaginary = (
        project(coupled_result[0], own_imaginary) - project(coupled_result[1], own_real)
    ) * scaling
    condensed_result = jnp.stack([compressed_real, compressed_imaginary]).astype(BF16)
    return (condensed_result, coupled_result)


def link_plain(ground, frames):
    dates, _, cells = ground.shape
    windows = frames.shape[0]
    extended = ground.reshape(dates, 2, HALO, cells)
    flat = extended.reshape(dates, 2, HALO * cells)
    readings = jnp.take(flat, frames.reshape(-1), axis=2).reshape(dates, 2, windows, LOOKS)
    native = extended[:, :, 1 : LB + 1].reshape(dates, 2, windows, LOOKS)
    condensed_result, coupled_result = coupling_frames(readings, native)
    history_real = coupled_result[0].astype(F32).T[:, :, None]
    history_imaginary = coupled_result[1].astype(F32).T[:, :, None]
    value_real = condensed_result[0].astype(F32)[None]
    value_imaginary = condensed_result[1].astype(F32)[None]
    rebuilt = jnp.stack(
        [
            value_real * history_real - value_imaginary * history_imaginary,
            value_real * history_imaginary + value_imaginary * history_real,
        ],
        axis=1,
    ).astype(BF16)
    return rebuilt.reshape(dates, 2 * LB, cells)


def dft_tables(length, span):
    first, second = np.arange(span)[:, None], np.arange(span)[None, :]
    angle = (first % length) * (second % length) % length * (2.0 * math.pi / length)
    inside = first // length == second // length
    return np.where(inside, np.cos(angle), 0.0), np.where(inside, np.sin(angle), 0.0)


def patch_kernel(range_table, ahead_table, back_table, mine, out, wide):
    blocks, _, cells = mine.shape
    chunks = cells // LANES

    def cut(value, j):
        return value[:, j * LANES : (j + 1) * LANES]

    for b in range(blocks):
        rows = mine[b].astype(F32)
        for j in range(chunks):
            wide[j, b * 2 * LB : (b + 1) * 2 * LB, :] = cut(rows, j)

    def lines_of(c, j):
        pieces = [wide[j, pl.ds(c * LB + t, blocks, stride=2 * LB), :] for t in range(LB)]
        return jnp.concatenate(pieces, axis=0).astype(BF16)

    first = jnp.concatenate(
        [
            jnp.concatenate([lines_of(0, j), lines_of(1, j)], axis=1)
            for j in range(chunks)
        ],
        axis=0,
    )

    def by_chunk(real, imaginary):
        return jnp.concatenate(
            [
                jnp.concatenate([cut(real, j), cut(imaginary, j)], axis=1)
                for j in range(chunks)
            ],
            axis=0,
        )

    def by_line(value, c):
        return jnp.concatenate(
            [cut(value[j * PATCH : (j + 1) * PATCH], c) for j in range(chunks)], axis=1
        )

    table = range_table[...]
    across = jnp.dot(first, table, preferred_element_type=F32).astype(BF16)
    across = jnp.concatenate([by_line(across, 0), by_line(across, 1)], axis=0)
    spectrum = jnp.dot(ahead_table[...], across, preferred_element_type=F32)
    real, imaginary = spectrum[:PATCH], spectrum[PATCH:]
    power = real * real + imaginary * imaginary
    total = jnp.sum(power, axis=0, keepdims=True)
    total = jnp.concatenate([cut(total, j) for j in range(chunks)], axis=0)
    lane = iota(total.shape, 1)
    shift = 1
    while shift < PATCH:
        other = jnp.where(
            (lane & shift) == 0, pltpu.roll(total, LANES - shift, 1), pltpu.roll(total, shift, 1)
        )
        total = total + other
        shift *= 2
    mean = total * (1.0 / (PATCH * PATCH)) + EPSILON
    mean = jnp.concatenate([mean[j : j + 1] for j in range(chunks)], axis=1)
    ramp = jnp.sqrt(jnp.sqrt(power / mean))
    weighted = jnp.concatenate([real * ramp, imaginary * ramp], axis=0).astype(BF16)
    back = jnp.dot(back_table[...], weighted, preferred_element_type=F32).astype(BF16)
    back = by_chunk(back[:PATCH], back[PATCH:])
    final = lax.dot_general(back, table, NT, preferred_element_type=F32)
    final = (final * (1.0 / (PATCH * PATCH))).astype(BF16)
    for c in range(2):
        out[0, c] = by_line(final, c)


def patch_filter(mine, lines):
    cells = mine.shape[2]
    blocks = PATCH // LB
    cosine, sine = dft_tables(PATCH, LANES)
    range_table = np.block([[cosine, -sine], [sine, cosine]])
    cosine, sine = dft_tables(PATCH, PATCH)
    order = np.arange(PATCH).reshape(blocks, LB).T.reshape(-1)
    ahead = np.block([[cosine[:, order], sine[:, order]], [-sine[:, order], cosine[:, order]]])
    back = np.block([[cosine, -sine], [sine, cosine]])
    tables = [jnp.asarray(entry, F32).astype(BF16) for entry in (range_table, ahead, back)]
    return pl.pallas_call(
        patch_kernel,
        grid=(lines // PATCH,),
        out_shape=jax.ShapeDtypeStruct((1, 2, lines, cells), BF16),
        in_specs=[
            pl.BlockSpec((2 * LANES, 2 * LANES), lambda p: (0, 0)),
            pl.BlockSpec((2 * PATCH, 2 * PATCH), lambda p: (0, 0)),
            pl.BlockSpec((2 * PATCH, 2 * PATCH), lambda p: (0, 0)),
            pl.BlockSpec((blocks, 2 * LB, cells), lambda p: (p, 0, 0)),
        ],
        out_specs=pl.BlockSpec((1, 2, PATCH, cells), lambda p: (0, 0, p, 0)),
        scratch_shapes=[pltpu.VMEM((cells // LANES, blocks * 2 * LB, LANES), F32)],
        compiler_params=grant(lines // LB),
    )(*tables, mine)


def on_device(
    salvo_records, stencil_weights, zone_drifts, seam_sweeps, prior_sweeps, viewing_frames
):
    devices = lax.axis_size("date")
    merged = seam(
        salvo_records, stencil_weights, zone_drifts, seam_sweeps, prior_sweeps, devices
    )
    ground = lax.all_to_all(merged, "date", split_axis=0, concat_axis=0, tiled=True)
    windows = viewing_frames.shape[0]
    fits = devices <= 32 and devices % 16 == 0 and LANES % windows == 0
    rebuilt = (link if fits else link_plain)(ground, viewing_frames)
    mine = lax.all_to_all(rebuilt, "date", split_axis=0, concat_axis=0, tiled=True)
    return patch_filter(mine, LB * devices)


def solution(mesh):
    in_specs = (
        P(("group", "date"), None, None, None, None),
        P(("group", "date"), None, None),
        P(("group", "date"), None),
        P(("group", "date"), None),
        P(("group", "date")),
        P(("group", "date"), None),
    )
    out_specs = P(("group", "date"), None, None, None)
    return jax.shard_map(
        on_device, mesh=mesh, in_specs=in_specs, out_specs=out_specs, check_vma=False
    )
```

```python
import functools
import math

import jax
import jax.numpy as jnp
import numpy as np
from jax import lax
from jax.experimental import pallas as pl
from jax.experimental.pallas import tpu as pltpu
from jax.sharding import PartitionSpec as P

LB = 2
SALVO_TALLY = 3
STENCIL_WEIGHTS = 8
LOOKS = 128
ITERS = 8
PATCH = 32
LANES = 128

EPSILON = 1e-06
SHRINK = 0.05

HALO = LB + 2
F32 = jnp.float32
BF16 = jnp.bfloat16
NT = (((1,), (1,)), ((), ()))


def iota(shape, axis):
    return lax.broadcasted_iota(jnp.int32, shape, axis)


def grant(devices):
    return pltpu.CompilerParams(vmem_limit_bytes=min(devices, 120) * 2**19)


def seam_kernel(*refs, sweep_labels):
    prior, sources, out = refs[0], refs[1:5], refs[5]
    (drifts, seams, weights, bursts), (wide, done) = refs[6:10], refs[10:]
    copies = [
        pltpu.make_async_copy(source, target, done.at[n])
        for n, (source, target) in enumerate(zip(sources, refs[6:10]))
    ]
    for copy in copies:
        copy.start()
    for copy in copies:
        copy.wait()
    sweeps, _, cells = bursts.shape[2:]
    slot = wide.shape[0] // SALVO_TALLY
    span = cells + LANES
    chunks = cells // LANES
    for b in range(SALVO_TALLY):
        for i in range(sweeps):
            wide[b * slot + 2 * i : b * slot + 2 * i + 2, :] = bursts[0, b, i].astype(F32)
        if 2 * sweeps < slot:
            wide[b * slot + 2 * sweeps : (b + 1) * slot, :] = jnp.zeros(
                (slot - 2 * sweeps, cells), F32
            )
    taps = weights[0].astype(F32)
    row, column = iota((LANES, LANES), 0), iota((LANES, LANES), 1)
    resampled = []
    for b in range(SALVO_TALLY):
        first = span + (STENCIL_WEIGHTS // 2 - 1) - drifts[0, b]
        first = jnp.where(first >= span, first - span, first)
        rotated = jnp.concatenate(
            [wide[b * slot : (b + 1) * slot, :], jnp.zeros((slot, LANES), F32)], axis=1
        )
        rotated = pltpu.roll(rotated, first, 1).astype(BF16)
        rotated = jnp.concatenate(
            [rotated[:, j * LANES : (j + 2) * LANES] for j in range(chunks)], axis=0
        )
        band = jnp.zeros((LANES, LANES), F32)
        for k in range(STENCIL_WEIGHTS):
            band = jnp.where(column == (LANES - k) % LANES, taps[b : b + 1, k : k + 1], band)
        band = pltpu.roll(band, 0, 1, stride=1, stride_axis=0)
        band = jnp.concatenate(
            [jnp.where(column <= row, band, 0.0), jnp.where(column > row, band, 0.0)], axis=0
        )
        total = jnp.dot(rotated, band.astype(BF16), preferred_element_type=F32).astype(BF16)
        resampled.append(
            jnp.concatenate([total[j * slot : (j + 1) * slot] for j in range(chunks)], axis=1)
        )
    shape = (out.shape[0] * 2 * HALO, SALVO_TALLY * slot)
    bits = slot.bit_length() - 1
    row, column = iota(shape, 0), iota(shape, 1)
    line = (row // (2 * HALO)) * LB - 1 + row % HALO
    part = (row // HALO) % 2
    which = lax.shift_right_logical(column, bits)
    entry = lax.shift_right_logical(column & (slot - 1), 1)
    place = jnp.zeros(shape, F32)
    start = -prior[0]
    for b in range(SALVO_TALLY):
        ramp = jnp.ones(shape, F32)
        if b > 0:
            start = start + sweeps - seams[0, b - 1]
            up = (line - start + 1).astype(F32) / (seams[0, b - 1] + 1).astype(F32)
            ramp = ramp * jnp.clip(up, 0.0, 1.0)
        if b < SALVO_TALLY - 1:
            down = (start + sweeps - line).astype(F32) / (seams[0, b] + 1).astype(F32)
            ramp = ramp * jnp.clip(down, 0.0, 1.0)
        place = jnp.where((which == b) & (line == start + entry), ramp, place)
    inside = (entry < sweeps) & (column & 1 == part) & (line >= 0) & (line < sweep_labels)
    place = jnp.where(inside, place, 0.0).astype(BF16)
    merged = jnp.dot(place, jnp.concatenate(resampled, axis=0), preferred_element_type=F32)
    out[...] = merged.reshape(out.shape).astype(BF16)


def seam(bursts, weights, drifts, seams, prior, devices):
    sweeps, cells = bursts.shape[3:]
    slot = 16
    while slot < 2 * sweeps:
        slot *= 2
    bursts = bursts.transpose(0, 1, 3, 2, 4)
    arrays = (drifts, seams, weights, bursts)
    return pl.pallas_call(
        functools.partial(seam_kernel, sweep_labels=LB * devices),
        out_shape=jax.ShapeDtypeStruct((devices, 2 * HALO, cells), BF16),
        in_specs=[
            pl.BlockSpec(memory_space=pltpu.SMEM),
            *[pl.BlockSpec(memory_space=pltpu.HBM)] * len(arrays),
        ],
        out_specs=pl.BlockSpec(memory_space=pltpu.VMEM),
        scratch_shapes=[
            pltpu.SMEM(drifts.shape, jnp.int32),
            pltpu.SMEM(seams.shape, jnp.int32),
            pltpu.VMEM(weights.shape, BF16),
            pltpu.VMEM(bursts.shape, BF16),
            pltpu.VMEM((SALVO_TALLY * slot, cells), F32),
            pltpu.SemaphoreType.DMA((len(arrays),)),
        ],
        compiler_params=grant(devices),
    )(prior, *[pltpu.with_memory_space_constraint(x, pltpu.HBM) for x in arrays])


def link_kernel(frames, ground, out, wide, table, left, right32, rebuilt):
    dates, _, cells = ground.shape
    windows = frames.shape[0]
    depth = 2 * dates
    span = depth * windows
    chunks = cells // LANES
    rows = ground[...].astype(F32).reshape(dates * 2 * HALO, cells)
    for j in range(chunks):
        wide[j] = rows[:, j * LANES : (j + 1) * LANES]

    def pixels(c, t, j):
        return wide[j, pl.ds(c * HALO + t, dates, stride=2 * HALO), :]

    segments = HALO * chunks // 2
    for t in range(HALO):
        for j in range(chunks):
            at = (t * (chunks // 2) + j // 2) * depth
            lanes = pl.ds((j % 2) * LANES, LANES)
            for c in range(2):
                table[at + c * dates : at + (c + 1) * dates, lanes] = pixels(c, t, j).astype(BF16)

    places = [
        (iota((16, LANES), 0) + 16 * n).astype(F32).astype(BF16) for n in range(2 * LANES // 16)
    ]
    one, zero = jnp.ones((16, LANES), BF16), jnp.zeros((16, LANES), BF16)
    for first in range(0, windows, 2):
        marks, highs = [], []
        for w in range(first, first + 2):
            pixel = frames[w : w + 1, :]
            low = jnp.broadcast_to(pixel & (2 * LANES - 1), (16, LANES)).astype(F32).astype(BF16)
            marks.append(
                jnp.concatenate([jnp.where(low == place, one, zero) for place in places], axis=0)
            )
            highs.append(lax.shift_right_logical(pixel, 8))
        high = jnp.broadcast_to(jnp.concatenate(highs, axis=1), (depth, 2 * LANES))
        taken = jnp.dot(
            table[...], jnp.concatenate(marks, axis=1), preferred_element_type=F32
        )
        found = taken[:depth]
        for s in range(1, segments):
            found = jnp.where(high == s, taken[s * depth : (s + 1) * depth], found)
        for w in range(first, first + 2):
            value = found[:, (w - first) * LANES : (w - first + 1) * LANES]
            turned = jnp.concatenate([-value[dates:], value[:dates]], axis=0)
            for half, piece in enumerate((value, turned)):
                left[w, :, half * LANES : (half + 1) * LANES] = piece.astype(BF16)
                right32[half, pl.ds(w, depth, stride=windows), :] = piece
    products = lax.dot_general(
        left[...].reshape(span, 2 * LANES),
        jnp.concatenate([right32[0], right32[1]], axis=1).astype(BF16),
        NT,
        preferred_element_type=F32,
    )
    owner = iota((depth, span), 1) & (windows - 1)
    cov = jnp.zeros((depth, span), F32)
    for w in range(windows):
        cov = jnp.where(owner == w, products[w * depth : (w + 1) * depth], cov)
    cov = cov * (1.0 / LOOKS)

    def over_lanes(value):
        total = value[:, :LANES]
        for j in range(1, span // LANES):
            total = total + value[:, j * LANES : (j + 1) * LANES]
        shift = windows
        while shift < LANES:
            total = total + pltpu.roll(total, shift, 1)
            shift *= 2
        return total

    def over_rows(value):
        return jnp.sum(value, axis=0, keepdims=True)

    def spread(value):
        return jnp.concatenate([value] * (span // LANES), axis=1)

    bits = windows.bit_length() - 1
    same = lax.shift_right_logical(iota((depth, span), 1), bits) == iota((depth, span), 0)
    diagonal = jnp.where(same, cov, 0.0)
    by_lane = lax.rsqrt(over_rows(diagonal) + EPSILON)
    by_row = lax.rsqrt(over_lanes(diagonal) + EPSILON)
    gam = (1.0 - SHRINK) * cov * spread(by_row) * by_lane + jnp.where(same, SHRINK, 0.0)

    y = jnp.where(iota((depth, LANES), 0) < dates, 1.0, 0.0)
    scale = jnp.ones((1, LANES), F32)
    for step in range(ITERS // 2):
        line = over_rows(gam * spread(y))
        size = over_lanes(line * line) * (1.0 / dates)
        scale = scale * lax.rsqrt(scale * scale * size + EPSILON)
        y = over_lanes(gam * line)
        size = over_rows(y * y) * (1.0 / dates)
        scale = scale * lax.rsqrt(scale * scale * size + EPSILON)
    linked = (y * scale).astype(BF16).astype(F32)

    factor = 1.0 / math.sqrt(dates)
    for w in range(windows):
        t, at = (w * LOOKS) // cells, (w * LOOKS) % cells
        column = jnp.broadcast_to(linked[:, w : w + 1], (depth, LANES))
        real, imaginary = column[:dates], column[dates:]
        own_real = pixels(0, 1 + t, at // LANES)
        own_imaginary = pixels(1, 1 + t, at // LANES)
        value_real = over_rows(real * own_real + imaginary * own_imaginary) * factor
        value_imaginary = over_rows(real * own_imaginary - imaginary * own_real) * factor
        value_real = value_real.astype(BF16).astype(F32)
        value_imaginary = value_imaginary.astype(BF16).astype(F32)
        rebuilt[at // LANES, pl.ds(t, dates, stride=2 * LB), :] = (
            value_real * real - value_imaginary * imaginary
        )
        rebuilt[at // LANES, pl.ds(LB + t, dates, stride=2 * LB), :] = (
            value_real * imaginary + value_imaginary * real
        )
    for d in range(dates):
        for j in range(chunks):
            out[d, :, j * LANES : (j + 1) * LANES] = rebuilt[
                j, d * 2 * LB : (d + 1) * 2 * LB, :
            ].astype(BF16)


def link(ground, frames):
    dates, _, cells = ground.shape
    windows = frames.shape[0]
    depth = 2 * dates
    vmem = pl.BlockSpec(memory_space=pltpu.VMEM)
    return pl.pallas_call(
        link_kernel,
        out_shape=jax.ShapeDtypeStruct((dates, 2 * LB, cells), BF16),
        in_specs=[vmem, vmem],
        out_specs=vmem,
        scratch_shapes=[
            pltpu.VMEM((cells // LANES, dates * 2 * HALO, LANES), F32),
            pltpu.VMEM((HALO * cells // (2 * LANES) * depth, 2 * LANES), BF16),
            pltpu.VMEM((windows, depth, 2 * LANES), BF16),
            pltpu.VMEM((2, depth * windows, LANES), F32),
            pltpu.VMEM((cells // LANES, dates * 2 * LB, LANES), F32),
        ],
        compiler_params=grant(dates),
    )(frames, ground)


def coupling_frames(readings, native_picture_elements):
    sample_real = readings[:, 0]
    sample_imaginary = readings[:, 1]

    def pair(left, right):
        return jnp.einsum("dwm,ewm->wde", left, right, preferred_element_type=F32)

    inverse_looks = 1.0 / LOOKS
    covariance_real = (
        pair(sample_real, sample_real) + pair(sample_imaginary, sample_imaginary)
    ) * inverse_looks
    mixed = pair(sample_imaginary, sample_real)
    covariance_imaginary = (mixed - jnp.swapaxes(mixed, 1, 2)) * inverse_looks
    dates = readings.shape[0]
    inverse_root = lax.rsqrt(jnp.diagonal(covariance_real, axis1=1, axis2=2) + EPSILON)
    outer = inverse_root[:, :, None] * inverse_root[:, None, :]
    identity = jnp.eye(dates, dtype=F32)
    coherence_real = (1.0 - SHRINK) * covariance_real * outer + SHRINK * identity
    coherence_imaginary = (1.0 - SHRINK) * covariance_imaginary * outer
    vector_real = jnp.ones(inverse_root.shape, F32)
    vector_imaginary = jnp.zeros(inverse_root.shape, F32)

    def apply_matrix(matrix, vector):
        return jnp.einsum("wde,we->wd", matrix, vector, precision=lax.Precision.HIGHEST)

    for iteration in range(ITERS):
        image_real = apply_matrix(coherence_real, vector_real) - apply_matrix(
            coherence_imaginary, vector_imaginary
        )
        image_imaginary = apply_matrix(coherence_real, vector_imaginary) + apply_matrix(
            coherence_imaginary, vector_real
        )
        power = image_real * image_real + image_imaginary * image_imaginary
        factor = lax.rsqrt(jnp.mean(power, axis=1, keepdims=True) + EPSILON)
        vector_real = image_real * factor
        vector_imaginary = image_imaginary * factor
    coupled_result = jnp.stack([vector_real, vector_imaginary]).astype(BF16)

    def project(history, pixels):
        return jnp.einsum("wd,dwm->wm", history, pixels, preferred_element_type=F32)

    scaling = 1.0 / math.sqrt(dates)
    own_real = native_picture_elements[:, 0]
    own_imaginary = native_picture_elements[:, 1]
    compressed_real = (
        project(coupled_result[0], own_real) + project(coupled_result[1], own_imaginary)
    ) * scaling
    compressed_imaginary = (
        project(coupled_result[0], own_imaginary) - project(coupled_result[1], own_real)
    ) * scaling
    condensed_result = jnp.stack([compressed_real, compressed_imaginary]).astype(BF16)
    return (condensed_result, coupled_result)


def link_plain(ground, frames):
    dates, _, cells = ground.shape
    windows = frames.shape[0]
    extended = ground.reshape(dates, 2, HALO, cells)
    flat = extended.reshape(dates, 2, HALO * cells)
    readings = jnp.take(flat, frames.reshape(-1), axis=2).reshape(dates, 2, windows, LOOKS)
    native = extended[:, :, 1 : LB + 1].reshape(dates, 2, windows, LOOKS)
    condensed_result, coupled_result = coupling_frames(readings, native)
    history_real = coupled_result[0].astype(F32).T[:, :, None]
    history_imaginary = coupled_result[1].astype(F32).T[:, :, None]
    value_real = condensed_result[0].astype(F32)[None]
    value_imaginary = condensed_result[1].astype(F32)[None]
    rebuilt = jnp.stack(
        [
            value_real * history_real - value_imaginary * history_imaginary,
            value_real * history_imaginary + value_imaginary * history_real,
        ],
        axis=1,
    ).astype(BF16)
    return rebuilt.reshape(dates, 2 * LB, cells)


def dft_tables(length, span):
    first, second = np.arange(span)[:, None], np.arange(span)[None, :]
    angle = (first % length) * (second % length) % length * (2.0 * math.pi / length)
    inside = first // length == second // length
    return np.where(inside, np.cos(angle), 0.0), np.where(inside, np.sin(angle), 0.0)


def patch_kernel(range_table, ahead_table, back_table, mine, out, wide):
    blocks, _, cells = mine.shape
    chunks = cells // LANES

    def cut(value, j):
        return value[:, j * LANES : (j + 1) * LANES]

    for b in range(blocks):
        rows = mine[b].astype(F32)
        for j in range(chunks):
            wide[j, b * 2 * LB : (b + 1) * 2 * LB, :] = cut(rows, j)

    def lines_of(c, j):
        pieces = [wide[j, pl.ds(c * LB + t, blocks, stride=2 * LB), :] for t in range(LB)]
        return jnp.concatenate(pieces, axis=0).astype(BF16)

    first = jnp.concatenate(
        [
            jnp.concatenate([lines_of(0, j), lines_of(1, j)], axis=1)
            for j in range(chunks)
        ],
        axis=0,
    )

    def by_chunk(real, imaginary):
        return jnp.concatenate(
            [
                jnp.concatenate([cut(real, j), cut(imaginary, j)], axis=1)
                for j in range(chunks)
            ],
            axis=0,
        )

    def by_line(value, c):
        return jnp.concatenate(
            [cut(value[j * PATCH : (j + 1) * PATCH], c) for j in range(chunks)], axis=1
        )

    table = range_table[...]
    across = jnp.dot(first, table, preferred_element_type=F32).astype(BF16)
    across = jnp.concatenate([by_line(across, 0), by_line(across, 1)], axis=0)
    spectrum = jnp.dot(ahead_table[...], across, preferred_element_type=F32)
    real, imaginary = spectrum[:PATCH], spectrum[PATCH:]
    power = real * real + imaginary * imaginary
    total = jnp.sum(power, axis=0, keepdims=True)
    total = jnp.concatenate([cut(total, j) for j in range(chunks)], axis=0)
    lane = iota(total.shape, 1)
    shift = 1
    while shift < PATCH:
        other = jnp.where(
            (lane & shift) == 0, pltpu.roll(total, LANES - shift, 1), pltpu.roll(total, shift, 1)
        )
        total = total + other
        shift *= 2
    mean = total * (1.0 / (PATCH * PATCH)) + EPSILON
    mean = jnp.concatenate([mean[j : j + 1] for j in range(chunks)], axis=1)
    ramp = jnp.sqrt(jnp.sqrt(power / mean))
    weighted = jnp.concatenate([real * ramp, imaginary * ramp], axis=0).astype(BF16)
    back = jnp.dot(back_table[...], weighted, preferred_element_type=F32).astype(BF16)
    back = by_chunk(back[:PATCH], back[PATCH:])
    final = lax.dot_general(back, table, NT, preferred_element_type=F32)
    final = (final * (1.0 / (PATCH * PATCH))).astype(BF16)
    for c in range(2):
        out[0, c] = by_line(final, c)


def patch_filter(mine, lines):
    cells = mine.shape[2]
    blocks = PATCH // LB
    cosine, sine = dft_tables(PATCH, LANES)
    range_table = np.block([[cosine, -sine], [sine, cosine]])
    cosine, sine = dft_tables(PATCH, PATCH)
    order = np.arange(PATCH).reshape(blocks, LB).T.reshape(-1)
    ahead = np.block([[cosine[:, order], sine[:, order]], [-sine[:, order], cosine[:, order]]])
    back = np.block([[cosine, -sine], [sine, cosine]])
    tables = [jnp.asarray(entry, F32).astype(BF16) for entry in (range_table, ahead, back)]
    return pl.pallas_call(
        patch_kernel,
        grid=(lines // PATCH,),
        out_shape=jax.ShapeDtypeStruct((1, 2, lines, cells), BF16),
        in_specs=[
            pl.BlockSpec((2 * LANES, 2 * LANES), lambda p: (0, 0)),
            pl.BlockSpec((2 * PATCH, 2 * PATCH), lambda p: (0, 0)),
            pl.BlockSpec((2 * PATCH, 2 * PATCH), lambda p: (0, 0)),
            pl.BlockSpec((blocks, 2 * LB, cells), lambda p: (p, 0, 0)),
        ],
        out_specs=pl.BlockSpec((1, 2, PATCH, cells), lambda p: (0, 0, p, 0)),
        scratch_shapes=[pltpu.VMEM((cells // LANES, blocks * 2 * LB, LANES), F32)],
        compiler_params=grant(lines // LB),
    )(*tables, mine)


def on_device(
    salvo_records, stencil_weights, zone_drifts, seam_sweeps, prior_sweeps, viewing_frames
):
    devices = lax.axis_size("date")
    merged = seam(
        salvo_records, stencil_weights, zone_drifts, seam_sweeps, prior_sweeps, devices
    )
    ground = lax.all_to_all(merged, "date", split_axis=0, concat_axis=0, tiled=True)
    windows = viewing_frames.shape[0]
    fits = devices <= 32 and devices % 16 == 0 and windows % 2 == 0 and LANES % windows == 0
    fits = fits and salvo_records.shape[4] % (2 * LANES) == 0
    rebuilt = (link if fits else link_plain)(ground, viewing_frames)
    mine = lax.all_to_all(rebuilt, "date", split_axis=0, concat_axis=0, tiled=True)
    return patch_filter(mine, LB * devices)


def solution(mesh):
    in_specs = (
        P(("group", "date"), None, None, None, None),
        P(("group", "date"), None, None),
        P(("group", "date"), None),
        P(("group", "date"), None),
        P(("group", "date")),
        P(("group", "date"), None),
    )
    out_specs = P(("group", "date"), None, None, None)
    return jax.shard_map(
        on_device, mesh=mesh, in_specs=in_specs, out_specs=out_specs, check_vma=False
    )
```

```python
import functools
import math

import jax
import jax.numpy as jnp
import numpy as np
from jax import lax
from jax.experimental import pallas as pl
from jax.experimental.pallas import tpu as pltpu
from jax.sharding import PartitionSpec as P

LB = 2
SALVO_TALLY = 3
STENCIL_WEIGHTS = 8
LOOKS = 128
ITERS = 8
PATCH = 32
LANES = 128
SEGMENT = 512
BATCH = 8

EPSILON = 1e-06
SHRINK = 0.05
SMALLEST = float(np.finfo(np.float32).tiny)

HALO = LB + 2
F32 = jnp.float32
BF16 = jnp.bfloat16
NT = (((1,), (1,)), ((), ()))


def iota(shape, axis):
    return lax.broadcasted_iota(jnp.int32, shape, axis)


def grant(devices):
    return pltpu.CompilerParams(vmem_limit_bytes=min(devices, 120) * 2**19)


def seam_kernel(*refs, sweep_labels):
    prior, sources, out = refs[0], refs[1:5], refs[5]
    (drifts, seams, weights, bursts), (wide, done) = refs[6:10], refs[10:]
    copies = [
        pltpu.make_async_copy(source, target, done.at[n])
        for n, (source, target) in enumerate(zip(sources, refs[6:10]))
    ]
    for copy in copies:
        copy.start()
    for copy in copies:
        copy.wait()
    sweeps, _, cells = bursts.shape[2:]
    slot = wide.shape[0] // SALVO_TALLY
    span = cells + LANES
    chunks = cells // LANES
    for b in range(SALVO_TALLY):
        for i in range(sweeps):
            wide[b * slot + 2 * i : b * slot + 2 * i + 2, :] = bursts[0, b, i].astype(F32)
        if 2 * sweeps < slot:
            wide[b * slot + 2 * sweeps : (b + 1) * slot, :] = jnp.zeros(
                (slot - 2 * sweeps, cells), F32
            )
    taps = weights[0].astype(F32)
    row, column = iota((LANES, LANES), 0), iota((LANES, LANES), 1)
    resampled = []
    for b in range(SALVO_TALLY):
        first = span + (STENCIL_WEIGHTS // 2 - 1) - drifts[0, b]
        first = jnp.where(first >= span, first - span, first)
        rotated = jnp.concatenate(
            [wide[b * slot : (b + 1) * slot, :], jnp.zeros((slot, LANES), F32)], axis=1
        )
        rotated = pltpu.roll(rotated, first, 1).astype(BF16)
        rotated = jnp.concatenate(
            [rotated[:, j * LANES : (j + 2) * LANES] for j in range(chunks)], axis=0
        )
        band = jnp.zeros((LANES, LANES), F32)
        for k in range(STENCIL_WEIGHTS):
            band = jnp.where(column == (LANES - k) % LANES, taps[b : b + 1, k : k + 1], band)
        band = pltpu.roll(band, 0, 1, stride=1, stride_axis=0)
        band = jnp.concatenate(
            [jnp.where(column <= row, band, 0.0), jnp.where(column > row, band, 0.0)], axis=0
        )
        total = jnp.dot(rotated, band.astype(BF16), preferred_element_type=F32).astype(BF16)
        resampled.append(
            jnp.concatenate([total[j * slot : (j + 1) * slot] for j in range(chunks)], axis=1)
        )
    shape = (out.shape[0] * 2 * HALO, SALVO_TALLY * slot)
    bits = slot.bit_length() - 1
    row, column = iota(shape, 0), iota(shape, 1)
    line = (row // (2 * HALO)) * LB - 1 + row % HALO
    part = (row // HALO) % 2
    which = lax.shift_right_logical(column, bits)
    entry = lax.shift_right_logical(column & (slot - 1), 1)
    place = jnp.zeros(shape, F32)
    start = -prior[0]
    for b in range(SALVO_TALLY):
        ramp = jnp.ones(shape, F32)
        if b > 0:
            start = start + sweeps - seams[0, b - 1]
            up = (line - start + 1).astype(F32) / (seams[0, b - 1] + 1).astype(F32)
            ramp = ramp * jnp.clip(up, 0.0, 1.0)
        if b < SALVO_TALLY - 1:
            down = (start + sweeps - line).astype(F32) / (seams[0, b] + 1).astype(F32)
            ramp = ramp * jnp.clip(down, 0.0, 1.0)
        place = jnp.where((which == b) & (line == start + entry), ramp, place)
    inside = (entry < sweeps) & (column & 1 == part) & (line >= 0) & (line < sweep_labels)
    place = jnp.where(inside, place, 0.0).astype(BF16)
    merged = jnp.dot(place, jnp.concatenate(resampled, axis=0), preferred_element_type=F32)
    out[...] = merged.reshape(out.shape).astype(BF16)


def seam(bursts, weights, drifts, seams, prior, devices):
    sweeps, cells = bursts.shape[3:]
    slot = 16
    while slot < 2 * sweeps:
        slot *= 2
    bursts = bursts.transpose(0, 1, 3, 2, 4)
    arrays = (drifts, seams, weights, bursts)
    return pl.pallas_call(
        functools.partial(seam_kernel, sweep_labels=LB * devices),
        out_shape=jax.ShapeDtypeStruct((devices, 2 * HALO, cells), BF16),
        in_specs=[
            pl.BlockSpec(memory_space=pltpu.SMEM),
            *[pl.BlockSpec(memory_space=pltpu.HBM)] * len(arrays),
        ],
        out_specs=pl.BlockSpec(memory_space=pltpu.VMEM),
        scratch_shapes=[
            pltpu.SMEM(drifts.shape, jnp.int32),
            pltpu.SMEM(seams.shape, jnp.int32),
            pltpu.VMEM(weights.shape, BF16),
            pltpu.VMEM(bursts.shape, BF16),
            pltpu.VMEM((SALVO_TALLY * slot, cells), F32),
            pltpu.SemaphoreType.DMA((len(arrays),)),
        ],
        compiler_params=grant(devices),
    )(prior, *[pltpu.with_memory_space_constraint(x, pltpu.HBM) for x in arrays])


def link_kernel(frames, ground, out, wide, right32, gam, rebuilt):
    dates, _, cells = ground.shape
    windows = frames.shape[0]
    depth = 2 * dates
    span = depth * windows
    chunks = cells // LANES
    pitch = 2 * HALO + 1
    for d in range(dates):
        rows = ground[d].astype(F32)
        for j in range(chunks):
            wide[j, d * pitch : d * pitch + 2 * HALO, :] = rows[:, j * LANES : (j + 1) * LANES]

    def pixels(c, t, j):
        return wide[j, pl.ds(c * HALO + t, dates, stride=pitch), :]

    per = SEGMENT // LANES
    segments = HALO * chunks // per
    table = jnp.concatenate(
        [
            jnp.concatenate(
                [
                    jnp.concatenate(
                        [pixels(c, *divmod(s * per + n, chunks)) for n in range(per)], axis=1
                    )
                    for c in range(2)
                ],
                axis=0,
            ).astype(BF16)
            for s in range(segments)
        ],
        axis=0,
    )

    half = SEGMENT // 2
    places = [(iota((16, LANES), 0) + 16 * n).astype(F32).astype(BF16) for n in range(half // 16)]
    one, zero = jnp.ones((16, LANES), BF16), jnp.zeros((16, LANES), BF16)

    values = []
    batch = min(BATCH, windows)
    for first in range(0, windows, batch):
        marks, highs = [], []
        for w in range(first, first + batch):
            pixel = frames[w : w + 1, :]
            low = pixel & (half - 1)
            upper = (pixel & half) == half
            keys = [jnp.where(upper, -1, low), jnp.where(upper, low, -1)]
            keys = [jnp.broadcast_to(key, (16, LANES)).astype(F32).astype(BF16) for key in keys]
            marks.append(
                jnp.concatenate(
                    [jnp.where(key == place, one, zero) for key in keys for place in places],
                    axis=0,
                )
            )
            highs.append(lax.shift_right_logical(pixel, SEGMENT.bit_length() - 1))
        high = jnp.broadcast_to(jnp.concatenate(highs, axis=1), (depth, batch * LANES))
        taken = jnp.dot(table, jnp.concatenate(marks, axis=1), preferred_element_type=F32)
        found = taken[:depth]
        for s in range(1, segments):
            found = jnp.where(high == s, taken[s * depth : (s + 1) * depth], found)
        values.extend(found[:, n * LANES : (n + 1) * LANES] for n in range(batch))
    left = []
    for w, value in enumerate(values):
        turned = jnp.concatenate([-value[dates:], value[:dates]], axis=0)
        left.append(jnp.concatenate([value[:dates], turned[:dates]], axis=1).astype(BF16))
        for n, piece in enumerate((value, turned)):
            right32[n, pl.ds(w, depth, stride=windows + 1), :] = piece
    products = lax.dot_general(
        jnp.concatenate(left, axis=0),
        jnp.concatenate(
            [
                jnp.concatenate(
                    [right32[n, at : at + windows].astype(BF16) for n in range(2)], axis=1
                )
                for at in range(0, depth * (windows + 1), windows + 1)
            ],
            axis=0,
        ),
        NT,
        preferred_element_type=F32,
    )
    owner = iota((dates, span), 1) & (windows - 1)
    cov = products[:dates]
    for w in range(1, windows):
        cov = jnp.where(owner == w, products[w * dates : (w + 1) * dates], cov)
    cov = cov * (1.0 / LOOKS)

    column = []
    for k in range(depth):
        tile, at = divmod(k * windows, LANES)
        entry = cov[:, tile * LANES : (tile + 1) * LANES]
        column.append(pltpu.roll(entry, LANES - at, 1) if at else entry)
    row = iota((dates, LANES), 0)
    power = column[0]
    for d in range(1, dates):
        power = jnp.where(row == d, column[d], power)
    inverse = lax.rsqrt(power + EPSILON)
    for k in range(depth):
        e = k % dates
        entry = (1.0 - SHRINK) * column[k] * inverse * inverse[e : e + 1]
        if k < dates:
            entry = entry + jnp.where(row == e, SHRINK, 0.0)
        gam[k] = entry

    def tree(terms):
        while len(terms) > 1:
            terms = [terms[n] + terms[n + 1] for n in range(0, len(terms), 2)]
        return terms[0]

    scale = jnp.ones((1, LANES), F32)
    real = tree([gam[e] for e in range(dates)])
    imaginary = -tree([gam[dates + e] for e in range(dates)])
    for step in range(ITERS):
        if step:
            reals = [real[e : e + 1] for e in range(dates)]
            imaginaries = [imaginary[e : e + 1] for e in range(dates)]
            real = tree(
                [gam[e] * reals[e] + gam[dates + e] * imaginaries[e] for e in range(dates)]
            )
            imaginary = tree(
                [gam[e] * imaginaries[e] - gam[dates + e] * reals[e] for e in range(dates)]
            )
        size = jnp.sum(real * real + imaginary * imaginary, axis=0, keepdims=True)
        scale = scale * lax.rsqrt(scale * scale * (size * (1.0 / dates)) + EPSILON)
    linked_real = (real * scale).astype(BF16).astype(F32)
    linked_imaginary = (imaginary * scale).astype(BF16).astype(F32)

    def over_rows(value):
        return jnp.sum(value, axis=0, keepdims=True)

    factor = 1.0 / math.sqrt(dates)
    for w in range(windows):
        t, at = (w * LOOKS) // cells, (w * LOOKS) % cells
        real = jnp.broadcast_to(linked_real[:, w : w + 1], (dates, LANES))
        imaginary = jnp.broadcast_to(linked_imaginary[:, w : w + 1], (dates, LANES))
        own_real = pixels(0, 1 + t, at // LANES)
        own_imaginary = pixels(1, 1 + t, at // LANES)
        value_real = over_rows(real * own_real + imaginary * own_imaginary) * factor
        value_imaginary = over_rows(real * own_imaginary - imaginary * own_real) * factor
        value_real = value_real.astype(BF16).astype(F32)
        value_imaginary = value_imaginary.astype(BF16).astype(F32)
        side, tile = divmod(at // LANES, chunks // 2)
        for c, value in enumerate(
            (
                value_real * real - value_imaginary * imaginary,
                value_real * imaginary + value_imaginary * real,
            )
        ):
            r = (c * LB + t) * 2 + side
            rebuilt[tile, pl.ds(r, dates, stride=4 * LB + 1), :] = value
    for d in range(dates):
        for j in range(chunks // 2):
            at = d * (4 * LB + 1)
            out[d, :, j * LANES : (j + 1) * LANES] = rebuilt[j, at : at + 4 * LB].astype(BF16)


def link(ground, frames):
    dates, _, cells = ground.shape
    windows = frames.shape[0]
    depth = 2 * dates
    vmem = pl.BlockSpec(memory_space=pltpu.VMEM)
    return pl.pallas_call(
        link_kernel,
        out_shape=jax.ShapeDtypeStruct((dates, 4 * LB, cells // 2), BF16),
        in_specs=[vmem, vmem],
        out_specs=vmem,
        scratch_shapes=[
            pltpu.VMEM((cells // LANES, dates * (2 * HALO + 1), LANES), F32),
            pltpu.VMEM((2, depth * (windows + 1), LANES), F32),
            pltpu.VMEM((depth, dates, LANES), F32),
            pltpu.VMEM((cells // (2 * LANES), dates * (4 * LB + 1), LANES), F32),
        ],
        compiler_params=grant(dates),
    )(frames, ground)


def coupling_frames(readings, native_picture_elements):
    sample_real = readings[:, 0]
    sample_imaginary = readings[:, 1]

    def pair(left, right):
        return jnp.einsum("dwm,ewm->wde", left, right, preferred_element_type=F32)

    inverse_looks = 1.0 / LOOKS
    covariance_real = (
        pair(sample_real, sample_real) + pair(sample_imaginary, sample_imaginary)
    ) * inverse_looks
    mixed = pair(sample_imaginary, sample_real)
    covariance_imaginary = (mixed - jnp.swapaxes(mixed, 1, 2)) * inverse_looks
    dates = readings.shape[0]
    inverse_root = lax.rsqrt(jnp.diagonal(covariance_real, axis1=1, axis2=2) + EPSILON)
    outer = inverse_root[:, :, None] * inverse_root[:, None, :]
    identity = jnp.eye(dates, dtype=F32)
    coherence_real = (1.0 - SHRINK) * covariance_real * outer + SHRINK * identity
    coherence_imaginary = (1.0 - SHRINK) * covariance_imaginary * outer
    vector_real = jnp.ones(inverse_root.shape, F32)
    vector_imaginary = jnp.zeros(inverse_root.shape, F32)

    def apply_matrix(matrix, vector):
        return jnp.einsum("wde,we->wd", matrix, vector, precision=lax.Precision.HIGHEST)

    for iteration in range(ITERS):
        image_real = apply_matrix(coherence_real, vector_real) - apply_matrix(
            coherence_imaginary, vector_imaginary
        )
        image_imaginary = apply_matrix(coherence_real, vector_imaginary) + apply_matrix(
            coherence_imaginary, vector_real
        )
        power = image_real * image_real + image_imaginary * image_imaginary
        factor = lax.rsqrt(jnp.mean(power, axis=1, keepdims=True) + EPSILON)
        vector_real = image_real * factor
        vector_imaginary = image_imaginary * factor
    coupled_result = jnp.stack([vector_real, vector_imaginary]).astype(BF16)

    def project(history, pixels):
        return jnp.einsum("wd,dwm->wm", history, pixels, preferred_element_type=F32)

    scaling = 1.0 / math.sqrt(dates)
    own_real = native_picture_elements[:, 0]
    own_imaginary = native_picture_elements[:, 1]
    compressed_real = (
        project(coupled_result[0], own_real) + project(coupled_result[1], own_imaginary)
    ) * scaling
    compressed_imaginary = (
        project(coupled_result[0], own_imaginary) - project(coupled_result[1], own_real)
    ) * scaling
    condensed_result = jnp.stack([compressed_real, compressed_imaginary]).astype(BF16)
    return (condensed_result, coupled_result)


def link_plain(ground, frames):
    dates, _, cells = ground.shape
    windows = frames.shape[0]
    extended = ground.reshape(dates, 2, HALO, cells)
    flat = extended.reshape(dates, 2, HALO * cells)
    readings = jnp.take(flat, frames.reshape(-1), axis=2).reshape(dates, 2, windows, LOOKS)
    native = extended[:, :, 1 : LB + 1].reshape(dates, 2, windows, LOOKS)
    condensed_result, coupled_result = coupling_frames(readings, native)
    history_real = coupled_result[0].astype(F32).T[:, :, None]
    history_imaginary = coupled_result[1].astype(F32).T[:, :, None]
    value_real = condensed_result[0].astype(F32)[None]
    value_imaginary = condensed_result[1].astype(F32)[None]
    rebuilt = jnp.stack(
        [
            value_real * history_real - value_imaginary * history_imaginary,
            value_real * history_imaginary + value_imaginary * history_real,
        ],
        axis=1,
    ).astype(BF16)
    return rebuilt.reshape(dates, 4 * LB, cells // 2)


def dft_tables(length, span):
    first, second = np.arange(span)[:, None], np.arange(span)[None, :]
    angle = (first % length) * (second % length) % length * (2.0 * math.pi / length)
    inside = first // length == second // length
    return np.where(inside, np.cos(angle), 0.0), np.where(inside, np.sin(angle), 0.0)


def patch_kernel(range_table, ahead_table, back_table, mine, out, wide):
    blocks, rows, _ = mine.shape
    cells = out.shape[3]
    chunks = cells // LANES

    def cut(value, j):
        return value[:, j * LANES : (j + 1) * LANES]

    for b in range(blocks):
        block = mine[b].astype(F32)
        for j in range(chunks // 2):
            wide[j, b * (rows + 1) : b * (rows + 1) + rows, :] = cut(block, j)

    def lines_of(c, j):
        side, j = divmod(j, chunks // 2)
        pieces = [
            wide[j, pl.ds((c * LB + t) * 2 + side, blocks, stride=rows + 1), :] for t in range(LB)
        ]
        return jnp.concatenate(pieces, axis=0).astype(BF16)

    first = jnp.concatenate(
        [
            jnp.concatenate([lines_of(0, j), lines_of(1, j)], axis=1)
            for j in range(chunks)
        ],
        axis=0,
    )

    def by_chunk(real, imaginary):
        return jnp.concatenate(
            [
                jnp.concatenate([cut(real, j), cut(imaginary, j)], axis=1)
                for j in range(chunks)
            ],
            axis=0,
        )

    def by_line(value, c):
        return jnp.concatenate(
            [cut(value[j * PATCH : (j + 1) * PATCH], c) for j in range(chunks)], axis=1
        )

    table = range_table[...]
    across = jnp.dot(first, table, preferred_element_type=F32).astype(BF16)
    across = jnp.concatenate([by_line(across, 0), by_line(across, 1)], axis=0)
    spectrum = jnp.dot(ahead_table[...], across, preferred_element_type=F32)
    real, imaginary = spectrum[:PATCH], spectrum[PATCH:]
    power = real * real + imaginary * imaginary
    total = jnp.sum(power, axis=0, keepdims=True)
    total = jnp.concatenate([cut(total, j) for j in range(chunks)], axis=0)
    pieces = []
    for _ in range(3):
        pieces.append(total.astype(BF16))
        total = total - pieces[-1].astype(F32)
    bits = PATCH.bit_length() - 1
    first, second = iota((LANES, LANES), 0), iota((LANES, LANES), 1)
    ones = lax.shift_right_logical(first, bits) == lax.shift_right_logical(second, bits)
    ones = jnp.where(ones, 1.0, 0.0).astype(BF16)
    pieces = jnp.concatenate(pieces, axis=0)
    pieces = jnp.dot(pieces, ones, preferred_element_type=F32)
    total = pieces[:chunks] + (pieces[chunks : 2 * chunks] + pieces[2 * chunks :])
    mean = total * (1.0 / (PATCH * PATCH)) + EPSILON
    mean = jnp.concatenate([mean[j : j + 1] for j in range(chunks)], axis=1)
    ramp = lax.rsqrt(lax.rsqrt(jnp.maximum(power / mean, SMALLEST)))
    weighted = jnp.concatenate([real * ramp, imaginary * ramp], axis=0).astype(BF16)
    back = jnp.dot(back_table[...], weighted, preferred_element_type=F32).astype(BF16)
    back = by_chunk(back[:PATCH], back[PATCH:])
    final = lax.dot_general(back, table, NT, preferred_element_type=F32)
    final = (final * (1.0 / (PATCH * PATCH))).astype(BF16)
    for c in range(2):
        out[0, c] = by_line(final, c)


def patch_filter(mine, lines):
    cells = 2 * mine.shape[2]
    blocks = PATCH // LB
    cosine, sine = dft_tables(PATCH, LANES)
    range_table = np.block([[cosine, -sine], [sine, cosine]])
    cosine, sine = dft_tables(PATCH, PATCH)
    order = np.arange(PATCH).reshape(blocks, LB).T.reshape(-1)
    ahead = np.block([[cosine[:, order], sine[:, order]], [-sine[:, order], cosine[:, order]]])
    back = np.block([[cosine, -sine], [sine, cosine]])
    tables = [jnp.asarray(entry, F32).astype(BF16) for entry in (range_table, ahead, back)]
    return pl.pallas_call(
        patch_kernel,
        grid=(lines // PATCH,),
        out_shape=jax.ShapeDtypeStruct((1, 2, lines, cells), BF16),
        in_specs=[
            pl.BlockSpec((2 * LANES, 2 * LANES), lambda p: (0, 0)),
            pl.BlockSpec((2 * PATCH, 2 * PATCH), lambda p: (0, 0)),
            pl.BlockSpec((2 * PATCH, 2 * PATCH), lambda p: (0, 0)),
            pl.BlockSpec((blocks, *mine.shape[1:]), lambda p: (p, 0, 0)),
        ],
        out_specs=pl.BlockSpec((1, 2, PATCH, cells), lambda p: (0, 0, p, 0)),
        scratch_shapes=[pltpu.VMEM((cells // (2 * LANES), blocks * (4 * LB + 1), LANES), F32)],
        compiler_params=grant(lines // LB),
    )(*tables, mine)


def on_device(
    salvo_records, stencil_weights, zone_drifts, seam_sweeps, prior_sweeps, viewing_frames
):
    devices = lax.axis_size("date")
    merged = seam(
        salvo_records, stencil_weights, zone_drifts, seam_sweeps, prior_sweeps, devices
    )
    ground = lax.all_to_all(merged, "date", split_axis=0, concat_axis=0, tiled=True)
    windows = viewing_frames.shape[0]
    fits = devices <= 32 and devices % 16 == 0 and windows % 2 == 0 and LANES % windows == 0
    fits = fits and salvo_records.shape[4] % SEGMENT == 0
    rebuilt = (link if fits else link_plain)(ground, viewing_frames)
    mine = lax.all_to_all(rebuilt, "date", split_axis=0, concat_axis=0, tiled=True)
    return patch_filter(mine, LB * devices)


def solution(mesh):
    in_specs = (
        P(("group", "date"), None, None, None, None),
        P(("group", "date"), None, None),
        P(("group", "date"), None),
        P(("group", "date"), None),
        P(("group", "date")),
        P(("group", "date"), None),
    )
    out_specs = P(("group", "date"), None, None, None)
    return jax.shard_map(
        on_device, mesh=mesh, in_specs=in_specs, out_specs=out_specs, check_vma=False
    )
```

```python
import functools
import math

import jax
import jax.numpy as jnp
import numpy as np
from jax import lax
from jax.experimental import pallas as pl
from jax.experimental.pallas import tpu as pltpu
from jax.sharding import PartitionSpec as P

LB = 2
SALVO_TALLY = 3
STENCIL_WEIGHTS = 8
LOOKS = 128
ITERS = 8
PATCH = 32
LANES = 128
SEGMENT = 512
BATCH = 8

EPSILON = 1e-06
SHRINK = 0.05
SMALLEST = float(np.finfo(np.float32).tiny)

HALO = LB + 2
F32 = jnp.float32
BF16 = jnp.bfloat16
NT = (((1,), (1,)), ((), ()))


def iota(shape, axis):
    return lax.broadcasted_iota(jnp.int32, shape, axis)


def grant(devices):
    return pltpu.CompilerParams(vmem_limit_bytes=min(devices, 120) * 2**19)


def early_kernel(out):
    out[...] = jnp.zeros(out.shape, F32)


def seam_kernel(prior, bursts, early, drifts, seams, weights, out, wide, *, sweep_labels):
    sweeps, _, cells = bursts.shape[2:]
    slot = wide.shape[0] // SALVO_TALLY
    span = cells + LANES
    chunks = cells // LANES
    for b in range(SALVO_TALLY):
        for i in range(sweeps):
            wide[b * slot + 2 * i : b * slot + 2 * i + 2, :] = bursts[0, b, i].astype(F32)
        if 2 * sweeps < slot:
            wide[b * slot + 2 * sweeps : (b + 1) * slot, :] = jnp.zeros(
                (slot - 2 * sweeps, cells), F32
            )
    taps = weights[0].astype(F32)
    row, column = iota((LANES, LANES), 0), iota((LANES, LANES), 1)
    resampled = []
    for b in range(SALVO_TALLY):
        first = span + (STENCIL_WEIGHTS // 2 - 1) - jnp.max(drifts[0:1, b : b + 1])
        first = jnp.where(first >= span, first - span, first)
        rotated = jnp.concatenate(
            [wide[b * slot : (b + 1) * slot, :], jnp.zeros((slot, LANES), F32)], axis=1
        )
        rotated = pltpu.roll(rotated, first, 1).astype(BF16)
        rotated = jnp.concatenate(
            [rotated[:, j * LANES : (j + 2) * LANES] for j in range(chunks)], axis=0
        )
        band = jnp.zeros((LANES, LANES), F32)
        for k in range(STENCIL_WEIGHTS):
            band = jnp.where(column == (LANES - k) % LANES, taps[b : b + 1, k : k + 1], band)
        band = pltpu.roll(band, 0, 1, stride=1, stride_axis=0)
        band = jnp.concatenate(
            [jnp.where(column <= row, band, 0.0), jnp.where(column > row, band, 0.0)], axis=0
        )
        total = jnp.dot(rotated, band.astype(BF16), preferred_element_type=F32).astype(BF16)
        resampled.append(
            jnp.concatenate([total[j * slot : (j + 1) * slot] for j in range(chunks)], axis=1)
        )
    shape = (out.shape[0] * 2 * HALO, SALVO_TALLY * slot)
    bits = slot.bit_length() - 1
    row, column = iota(shape, 0), iota(shape, 1)
    line = (row // (2 * HALO)) * LB - 1 + row % HALO
    part = (row // HALO) % 2
    which = lax.shift_right_logical(column, bits)
    entry = lax.shift_right_logical(column & (slot - 1), 1)
    place = jnp.zeros(shape, F32)
    start = -prior[0]
    for b in range(SALVO_TALLY):
        ramp = jnp.ones(shape, F32)
        if b > 0:
            start = start + sweeps - seams[0:1, b - 1 : b]
            up = (line - start + 1).astype(F32) / (seams[0:1, b - 1 : b] + 1).astype(F32)
            ramp = ramp * jnp.clip(up, 0.0, 1.0)
        if b < SALVO_TALLY - 1:
            down = (start + sweeps - line).astype(F32) / (seams[0:1, b : b + 1] + 1).astype(F32)
            ramp = ramp * jnp.clip(down, 0.0, 1.0)
        place = jnp.where((which == b) & (line == start + entry), ramp, place)
    inside = (entry < sweeps) & (column & 1 == part) & (line >= 0) & (line < sweep_labels)
    place = jnp.where(inside, place, 0.0).astype(BF16)
    merged = jnp.dot(place, jnp.concatenate(resampled, axis=0), preferred_element_type=F32)
    out[...] = merged.reshape(out.shape).astype(BF16)


def seam(bursts, weights, drifts, seams, prior, devices):
    sweeps, cells = bursts.shape[3:]
    slot = 16
    while slot < 2 * sweeps:
        slot *= 2
    bursts = bursts.transpose(0, 1, 3, 2, 4)
    early = pl.pallas_call(
        early_kernel,
        out_shape=jax.ShapeDtypeStruct((8, LANES), F32),
        compiler_params=grant(devices),
        cost_estimate=pl.CostEstimate(flops=10**8, bytes_accessed=4096, transcendentals=0),
    )()
    return pl.pallas_call(
        functools.partial(seam_kernel, sweep_labels=LB * devices),
        out_shape=jax.ShapeDtypeStruct((devices, 2 * HALO, cells), BF16),
        in_specs=[
            pl.BlockSpec(memory_space=pltpu.SMEM),
            *[pl.BlockSpec(memory_space=pltpu.VMEM)] * 5,
        ],
        out_specs=pl.BlockSpec(memory_space=pltpu.VMEM),
        scratch_shapes=[
            pltpu.VMEM((SALVO_TALLY * slot, cells), F32),
        ],
        compiler_params=grant(devices),
    )(prior, bursts, early, drifts, seams, weights)


def link_kernel(frames, ground, out, wide, right32, gam, rebuilt):
    dates, _, cells = ground.shape
    windows = frames.shape[0]
    depth = 2 * dates
    span = depth * windows
    chunks = cells // LANES
    pitch = 2 * HALO + 1
    for d in range(dates):
        rows = ground[d].astype(F32)
        for j in range(chunks):
            wide[j, d * pitch : d * pitch + 2 * HALO, :] = rows[:, j * LANES : (j + 1) * LANES]

    def pixels(c, t, j):
        return wide[j, pl.ds(c * HALO + t, dates, stride=pitch), :]

    per = SEGMENT // LANES
    segments = HALO * chunks // per
    table = jnp.concatenate(
        [
            jnp.concatenate(
                [
                    jnp.concatenate(
                        [pixels(c, *divmod(s * per + n, chunks)) for n in range(per)], axis=1
                    )
                    for c in range(2)
                ],
                axis=0,
            ).astype(BF16)
            for s in range(segments)
        ],
        axis=0,
    )

    half = SEGMENT // 2
    places = [(iota((16, LANES), 0) + 16 * n).astype(F32).astype(BF16) for n in range(half // 16)]
    one, zero = jnp.ones((16, LANES), BF16), jnp.zeros((16, LANES), BF16)

    values = []
    batch = min(BATCH, windows)
    for first in range(0, windows, batch):
        marks, highs = [], []
        for w in range(first, first + batch):
            pixel = frames[w : w + 1, :]
            low = pixel & (half - 1)
            upper = (pixel & half) == half
            keys = [jnp.where(upper, -1, low), jnp.where(upper, low, -1)]
            keys = [jnp.broadcast_to(key, (16, LANES)).astype(F32).astype(BF16) for key in keys]
            marks.append(
                jnp.concatenate(
                    [jnp.where(key == place, one, zero) for key in keys for place in places],
                    axis=0,
                )
            )
            highs.append(lax.shift_right_logical(pixel, SEGMENT.bit_length() - 1))
        high = jnp.broadcast_to(jnp.concatenate(highs, axis=1), (depth, batch * LANES))
        taken = jnp.dot(table, jnp.concatenate(marks, axis=1), preferred_element_type=F32)
        found = taken[:depth]
        for s in range(1, segments):
            found = jnp.where(high == s, taken[s * depth : (s + 1) * depth], found)
        values.extend(found[:, n * LANES : (n + 1) * LANES] for n in range(batch))
    left = []
    for w, value in enumerate(values):
        turned = jnp.concatenate([-value[dates:], value[:dates]], axis=0)
        left.append(jnp.concatenate([value[:dates], turned[:dates]], axis=1).astype(BF16))
        for n, piece in enumerate((value, turned)):
            right32[n, pl.ds(w, depth, stride=windows + 1), :] = piece
    products = lax.dot_general(
        jnp.concatenate(left, axis=0),
        jnp.concatenate(
            [
                jnp.concatenate(
                    [right32[n, at : at + windows].astype(BF16) for n in range(2)], axis=1
                )
                for at in range(0, depth * (windows + 1), windows + 1)
            ],
            axis=0,
        ),
        NT,
        preferred_element_type=F32,
    )
    owner = iota((dates, span), 1) & (windows - 1)
    cov = products[:dates]
    for w in range(1, windows):
        cov = jnp.where(owner == w, products[w * dates : (w + 1) * dates], cov)
    cov = cov * (1.0 / LOOKS)

    column = []
    for k in range(depth):
        tile, at = divmod(k * windows, LANES)
        entry = cov[:, tile * LANES : (tile + 1) * LANES]
        column.append(pltpu.roll(entry, LANES - at, 1) if at else entry)
    row = iota((dates, LANES), 0)
    power = column[0]
    for d in range(1, dates):
        power = jnp.where(row == d, column[d], power)
    inverse = lax.rsqrt(power + EPSILON)
    for k in range(depth):
        e = k % dates
        entry = (1.0 - SHRINK) * column[k] * inverse * inverse[e : e + 1]
        if k < dates:
            entry = entry + jnp.where(row == e, SHRINK, 0.0)
        gam[k] = entry

    def tree(terms):
        while len(terms) > 1:
            terms = [terms[n] + terms[n + 1] for n in range(0, len(terms), 2)]
        return terms[0]

    scale = jnp.ones((1, LANES), F32)
    real = tree([gam[e] for e in range(dates)])
    imaginary = -tree([gam[dates + e] for e in range(dates)])
    for step in range(ITERS):
        if step:
            reals = [real[e : e + 1] for e in range(dates)]
            imaginaries = [imaginary[e : e + 1] for e in range(dates)]
            real = tree(
                [gam[e] * reals[e] + gam[dates + e] * imaginaries[e] for e in range(dates)]
            )
            imaginary = tree(
                [gam[e] * imaginaries[e] - gam[dates + e] * reals[e] for e in range(dates)]
            )
        size = jnp.sum(real * real + imaginary * imaginary, axis=0, keepdims=True)
        scale = scale * lax.rsqrt(scale * scale * (size * (1.0 / dates)) + EPSILON)
    linked_real = (real * scale).astype(BF16).astype(F32)
    linked_imaginary = (imaginary * scale).astype(BF16).astype(F32)

    def over_rows(value):
        return jnp.sum(value, axis=0, keepdims=True)

    factor = 1.0 / math.sqrt(dates)
    for w in range(windows):
        t, at = (w * LOOKS) // cells, (w * LOOKS) % cells
        real = jnp.broadcast_to(linked_real[:, w : w + 1], (dates, LANES))
        imaginary = jnp.broadcast_to(linked_imaginary[:, w : w + 1], (dates, LANES))
        own_real = pixels(0, 1 + t, at // LANES)
        own_imaginary = pixels(1, 1 + t, at // LANES)
        value_real = over_rows(real * own_real + imaginary * own_imaginary) * factor
        value_imaginary = over_rows(real * own_imaginary - imaginary * own_real) * factor
        value_real = value_real.astype(BF16).astype(F32)
        value_imaginary = value_imaginary.astype(BF16).astype(F32)
        side, tile = divmod(at // LANES, chunks // 2)
        for c, value in enumerate(
            (
                value_real * real - value_imaginary * imaginary,
                value_real * imaginary + value_imaginary * real,
            )
        ):
            r = (c * LB + t) * 2 + side
            rebuilt[tile, pl.ds(r, dates, stride=4 * LB + 1), :] = value
    for d in range(dates):
        for j in range(chunks // 2):
            at = d * (4 * LB + 1)
            out[d, :, j * LANES : (j + 1) * LANES] = rebuilt[j, at : at + 4 * LB].astype(BF16)


def link(ground, frames):
    dates, _, cells = ground.shape
    windows = frames.shape[0]
    depth = 2 * dates
    vmem = pl.BlockSpec(memory_space=pltpu.VMEM)
    return pl.pallas_call(
        link_kernel,
        out_shape=jax.ShapeDtypeStruct((dates, 4 * LB, cells // 2), BF16),
        in_specs=[vmem, vmem],
        out_specs=vmem,
        scratch_shapes=[
            pltpu.VMEM((cells // LANES, dates * (2 * HALO + 1), LANES), F32),
            pltpu.VMEM((2, depth * (windows + 1), LANES), F32),
            pltpu.VMEM((depth, dates, LANES), F32),
            pltpu.VMEM((cells // (2 * LANES), dates * (4 * LB + 1), LANES), F32),
        ],
        compiler_params=grant(dates),
    )(frames, ground)


def coupling_frames(readings, native_picture_elements):
    sample_real = readings[:, 0]
    sample_imaginary = readings[:, 1]

    def pair(left, right):
        return jnp.einsum("dwm,ewm->wde", left, right, preferred_element_type=F32)

    inverse_looks = 1.0 / LOOKS
    covariance_real = (
        pair(sample_real, sample_real) + pair(sample_imaginary, sample_imaginary)
    ) * inverse_looks
    mixed = pair(sample_imaginary, sample_real)
    covariance_imaginary = (mixed - jnp.swapaxes(mixed, 1, 2)) * inverse_looks
    dates = readings.shape[0]
    inverse_root = lax.rsqrt(jnp.diagonal(covariance_real, axis1=1, axis2=2) + EPSILON)
    outer = inverse_root[:, :, None] * inverse_root[:, None, :]
    identity = jnp.eye(dates, dtype=F32)
    coherence_real = (1.0 - SHRINK) * covariance_real * outer + SHRINK * identity
    coherence_imaginary = (1.0 - SHRINK) * covariance_imaginary * outer
    vector_real = jnp.ones(inverse_root.shape, F32)
    vector_imaginary = jnp.zeros(inverse_root.shape, F32)

    def apply_matrix(matrix, vector):
        return jnp.einsum("wde,we->wd", matrix, vector, precision=lax.Precision.HIGHEST)

    for iteration in range(ITERS):
        image_real = apply_matrix(coherence_real, vector_real) - apply_matrix(
            coherence_imaginary, vector_imaginary
        )
        image_imaginary = apply_matrix(coherence_real, vector_imaginary) + apply_matrix(
            coherence_imaginary, vector_real
        )
        power = image_real * image_real + image_imaginary * image_imaginary
        factor = lax.rsqrt(jnp.mean(power, axis=1, keepdims=True) + EPSILON)
        vector_real = image_real * factor
        vector_imaginary = image_imaginary * factor
    coupled_result = jnp.stack([vector_real, vector_imaginary]).astype(BF16)

    def project(history, pixels):
        return jnp.einsum("wd,dwm->wm", history, pixels, preferred_element_type=F32)

    scaling = 1.0 / math.sqrt(dates)
    own_real = native_picture_elements[:, 0]
    own_imaginary = native_picture_elements[:, 1]
    compressed_real = (
        project(coupled_result[0], own_real) + project(coupled_result[1], own_imaginary)
    ) * scaling
    compressed_imaginary = (
        project(coupled_result[0], own_imaginary) - project(coupled_result[1], own_real)
    ) * scaling
    condensed_result = jnp.stack([compressed_real, compressed_imaginary]).astype(BF16)
    return (condensed_result, coupled_result)


def link_plain(ground, frames):
    dates, _, cells = ground.shape
    windows = frames.shape[0]
    extended = ground.reshape(dates, 2, HALO, cells)
    flat = extended.reshape(dates, 2, HALO * cells)
    readings = jnp.take(flat, frames.reshape(-1), axis=2).reshape(dates, 2, windows, LOOKS)
    native = extended[:, :, 1 : LB + 1].reshape(dates, 2, windows, LOOKS)
    condensed_result, coupled_result = coupling_frames(readings, native)
    history_real = coupled_result[0].astype(F32).T[:, :, None]
    history_imaginary = coupled_result[1].astype(F32).T[:, :, None]
    value_real = condensed_result[0].astype(F32)[None]
    value_imaginary = condensed_result[1].astype(F32)[None]
    rebuilt = jnp.stack(
        [
            value_real * history_real - value_imaginary * history_imaginary,
            value_real * history_imaginary + value_imaginary * history_real,
        ],
        axis=1,
    ).astype(BF16)
    return rebuilt.reshape(dates, 4 * LB, cells // 2)


def dft_tables(length, span):
    first, second = np.arange(span)[:, None], np.arange(span)[None, :]
    angle = (first % length) * (second % length) % length * (2.0 * math.pi / length)
    inside = first // length == second // length
    return np.where(inside, np.cos(angle), 0.0), np.where(inside, np.sin(angle), 0.0)


def patch_kernel(range_table, ahead_table, back_table, mine, out, wide):
    blocks, rows, _ = mine.shape
    cells = out.shape[3]
    chunks = cells // LANES

    def cut(value, j):
        return value[:, j * LANES : (j + 1) * LANES]

    for b in range(blocks):
        block = mine[b].astype(F32)
        for j in range(chunks // 2):
            wide[j, b * (rows + 1) : b * (rows + 1) + rows, :] = cut(block, j)

    def lines_of(c, j):
        side, j = divmod(j, chunks // 2)
        pieces = [
            wide[j, pl.ds((c * LB + t) * 2 + side, blocks, stride=rows + 1), :] for t in range(LB)
        ]
        return jnp.concatenate(pieces, axis=0).astype(BF16)

    first = jnp.concatenate(
        [
            jnp.concatenate([lines_of(0, j), lines_of(1, j)], axis=1)
            for j in range(chunks)
        ],
        axis=0,
    )

    def by_chunk(real, imaginary):
        return jnp.concatenate(
            [
                jnp.concatenate([cut(real, j), cut(imaginary, j)], axis=1)
                for j in range(chunks)
            ],
            axis=0,
        )

    def by_line(value, c):
        return jnp.concatenate(
            [cut(value[j * PATCH : (j + 1) * PATCH], c) for j in range(chunks)], axis=1
        )

    table = range_table[...]
    across = jnp.dot(first, table, preferred_element_type=F32).astype(BF16)
    across = jnp.concatenate([by_line(across, 0), by_line(across, 1)], axis=0)
    spectrum = jnp.dot(ahead_table[...], across, preferred_element_type=F32)
    real, imaginary = spectrum[:PATCH], spectrum[PATCH:]
    power = real * real + imaginary * imaginary
    total = jnp.sum(power, axis=0, keepdims=True)
    total = jnp.concatenate([cut(total, j) for j in range(chunks)], axis=0)
    pieces = []
    for _ in range(3):
        pieces.append(total.astype(BF16))
        total = total - pieces[-1].astype(F32)
    bits = PATCH.bit_length() - 1
    first, second = iota((LANES, LANES), 0), iota((LANES, LANES), 1)
    ones = lax.shift_right_logical(first, bits) == lax.shift_right_logical(second, bits)
    ones = jnp.where(ones, 1.0, 0.0).astype(BF16)
    pieces = jnp.concatenate(pieces, axis=0)
    pieces = jnp.dot(pieces, ones, preferred_element_type=F32)
    total = pieces[:chunks] + (pieces[chunks : 2 * chunks] + pieces[2 * chunks :])
    mean = total * (1.0 / (PATCH * PATCH)) + EPSILON
    mean = jnp.concatenate([mean[j : j + 1] for j in range(chunks)], axis=1)
    ramp = lax.rsqrt(lax.rsqrt(jnp.maximum(power / mean, SMALLEST)))
    weighted = jnp.concatenate([real * ramp, imaginary * ramp], axis=0).astype(BF16)
    back = jnp.dot(back_table[...], weighted, preferred_element_type=F32).astype(BF16)
    back = by_chunk(back[:PATCH], back[PATCH:])
    final = lax.dot_general(back, table, NT, preferred_element_type=F32)
    final = (final * (1.0 / (PATCH * PATCH))).astype(BF16)
    for c in range(2):
        out[0, c] = by_line(final, c)


def patch_filter(mine, lines):
    cells = 2 * mine.shape[2]
    blocks = PATCH // LB
    cosine, sine = dft_tables(PATCH, LANES)
    range_table = np.block([[cosine, -sine], [sine, cosine]])
    cosine, sine = dft_tables(PATCH, PATCH)
    order = np.arange(PATCH).reshape(blocks, LB).T.reshape(-1)
    ahead = np.block([[cosine[:, order], sine[:, order]], [-sine[:, order], cosine[:, order]]])
    back = np.block([[cosine, -sine], [sine, cosine]])
    tables = [jnp.asarray(entry, F32).astype(BF16) for entry in (range_table, ahead, back)]
    return pl.pallas_call(
        patch_kernel,
        grid=(lines // PATCH,),
        out_shape=jax.ShapeDtypeStruct((1, 2, lines, cells), BF16),
        in_specs=[
            pl.BlockSpec((2 * LANES, 2 * LANES), lambda p: (0, 0)),
            pl.BlockSpec((2 * PATCH, 2 * PATCH), lambda p: (0, 0)),
            pl.BlockSpec((2 * PATCH, 2 * PATCH), lambda p: (0, 0)),
            pl.BlockSpec((blocks, *mine.shape[1:]), lambda p: (p, 0, 0)),
        ],
        out_specs=pl.BlockSpec((1, 2, PATCH, cells), lambda p: (0, 0, p, 0)),
        scratch_shapes=[pltpu.VMEM((cells // (2 * LANES), blocks * (4 * LB + 1), LANES), F32)],
        compiler_params=grant(lines // LB),
    )(*tables, mine)


def on_device(
    salvo_records, stencil_weights, zone_drifts, seam_sweeps, prior_sweeps, viewing_frames
):
    devices = lax.axis_size("date")
    merged = seam(
        salvo_records, stencil_weights, zone_drifts, seam_sweeps, prior_sweeps, devices
    )
    ground = lax.all_to_all(merged, "date", split_axis=0, concat_axis=0, tiled=True)
    windows = viewing_frames.shape[0]
    fits = devices <= 32 and devices % 16 == 0 and windows % 2 == 0 and LANES % windows == 0
    fits = fits and salvo_records.shape[4] % SEGMENT == 0
    rebuilt = (link if fits else link_plain)(ground, viewing_frames)
    mine = lax.all_to_all(rebuilt, "date", split_axis=0, concat_axis=0, tiled=True)
    return patch_filter(mine, LB * devices)


def solution(mesh):
    in_specs = (
        P(("group", "date"), None, None, None, None),
        P(("group", "date"), None, None),
        P(("group", "date"), None),
        P(("group", "date"), None),
        P(("group", "date")),
        P(("group", "date"), None),
    )
    out_specs = P(("group", "date"), None, None, None)
    return jax.shard_map(
        on_device, mesh=mesh, in_specs=in_specs, out_specs=out_specs, check_vma=False
    )
```

```python
import functools
import math

import jax
import jax.numpy as jnp
import numpy as np
from jax import lax
from jax.experimental import pallas as pl
from jax.experimental.pallas import tpu as pltpu
from jax.sharding import PartitionSpec as P

LB = 2
SALVO_TALLY = 3
STENCIL_WEIGHTS = 8
LOOKS = 128
ITERS = 8
PATCH = 32
LANES = 128
SEGMENT = 256
BATCH = 8

EPSILON = 1e-06
SHRINK = 0.05
SMALLEST = float(np.finfo(np.float32).tiny)

HALO = LB + 2
F32 = jnp.float32
BF16 = jnp.bfloat16
NT = (((1,), (1,)), ((), ()))


def iota(shape, axis):
    return lax.broadcasted_iota(jnp.int32, shape, axis)


def grant(devices):
    return pltpu.CompilerParams(vmem_limit_bytes=min(devices, 120) * 2**19)


def early_kernel(out):
    out[...] = jnp.zeros(out.shape, F32)


def seam_kernel(prior, bursts, early, drifts, seams, weights, out, wide, *, sweep_labels):
    sweeps, _, cells = bursts.shape[2:]
    slot = wide.shape[0] // SALVO_TALLY
    span = cells + LANES
    chunks = cells // LANES
    for b in range(SALVO_TALLY):
        for i in range(sweeps):
            wide[b * slot + 2 * i : b * slot + 2 * i + 2, :] = bursts[0, b, i].astype(F32)
        if 2 * sweeps < slot:
            wide[b * slot + 2 * sweeps : (b + 1) * slot, :] = jnp.zeros(
                (slot - 2 * sweeps, cells), F32
            )
    taps = weights[0].astype(F32)
    row, column = iota((LANES, LANES), 0), iota((LANES, LANES), 1)
    resampled = []
    for b in range(SALVO_TALLY):
        first = span + (STENCIL_WEIGHTS // 2 - 1) - jnp.max(drifts[0:1, b : b + 1])
        first = jnp.where(first >= span, first - span, first)
        rotated = jnp.concatenate(
            [wide[b * slot : (b + 1) * slot, :], jnp.zeros((slot, LANES), F32)], axis=1
        )
        rotated = pltpu.roll(rotated, first, 1).astype(BF16)
        rotated = jnp.concatenate(
            [rotated[:, j * LANES : (j + 2) * LANES] for j in range(chunks)], axis=0
        )
        band = jnp.zeros((LANES, LANES), F32)
        for k in range(STENCIL_WEIGHTS):
            band = jnp.where(column == (LANES - k) % LANES, taps[b : b + 1, k : k + 1], band)
        band = pltpu.roll(band, 0, 1, stride=1, stride_axis=0)
        band = jnp.concatenate(
            [jnp.where(column <= row, band, 0.0), jnp.where(column > row, band, 0.0)], axis=0
        )
        total = jnp.dot(rotated, band.astype(BF16), preferred_element_type=F32).astype(BF16)
        resampled.append(
            jnp.concatenate([total[j * slot : (j + 1) * slot] for j in range(chunks)], axis=1)
        )
    shape = (out.shape[0] * 2 * HALO, SALVO_TALLY * slot)
    bits = slot.bit_length() - 1
    row, column = iota(shape, 0), iota(shape, 1)
    line = (row // (2 * HALO)) * LB - 1 + row % HALO
    part = (row // HALO) % 2
    which = lax.shift_right_logical(column, bits)
    entry = lax.shift_right_logical(column & (slot - 1), 1)
    place = jnp.zeros(shape, F32)
    start = -prior[0]
    for b in range(SALVO_TALLY):
        ramp = jnp.ones(shape, F32)
        if b > 0:
            start = start + sweeps - seams[0:1, b - 1 : b]
            up = (line - start + 1).astype(F32) / (seams[0:1, b - 1 : b] + 1).astype(F32)
            ramp = ramp * jnp.clip(up, 0.0, 1.0)
        if b < SALVO_TALLY - 1:
            down = (start + sweeps - line).astype(F32) / (seams[0:1, b : b + 1] + 1).astype(F32)
            ramp = ramp * jnp.clip(down, 0.0, 1.0)
        place = jnp.where((which == b) & (line == start + entry), ramp, place)
    inside = (entry < sweeps) & (column & 1 == part) & (line >= 0) & (line < sweep_labels)
    place = jnp.where(inside, place, 0.0).astype(BF16)
    merged = jnp.dot(place, jnp.concatenate(resampled, axis=0), preferred_element_type=F32)
    out[...] = merged.reshape(out.shape).astype(BF16)


def seam(bursts, weights, drifts, seams, prior, devices):
    sweeps, cells = bursts.shape[3:]
    slot = 16
    while slot < 2 * sweeps:
        slot *= 2
    bursts = bursts.transpose(0, 1, 3, 2, 4)
    early = pl.pallas_call(
        early_kernel,
        out_shape=jax.ShapeDtypeStruct((8, LANES), F32),
        compiler_params=grant(devices),
        cost_estimate=pl.CostEstimate(flops=10**8, bytes_accessed=4096, transcendentals=0),
    )()
    return pl.pallas_call(
        functools.partial(seam_kernel, sweep_labels=LB * devices),
        out_shape=jax.ShapeDtypeStruct((devices, 2 * HALO, cells), BF16),
        in_specs=[
            pl.BlockSpec(memory_space=pltpu.SMEM),
            *[pl.BlockSpec(memory_space=pltpu.VMEM)] * 5,
        ],
        out_specs=pl.BlockSpec(memory_space=pltpu.VMEM),
        scratch_shapes=[
            pltpu.VMEM((SALVO_TALLY * slot, cells), F32),
        ],
        compiler_params=grant(devices),
    )(prior, bursts, early, drifts, seams, weights)


def link_kernel(frames, ground, out, wide, right32, gam, rebuilt):
    dates, _, cells = ground.shape
    windows = frames.shape[0]
    depth = 2 * dates
    span = depth * windows
    chunks = cells // LANES
    pitch = 2 * HALO + 1
    for d in range(dates):
        rows = ground[d].astype(F32)
        for j in range(chunks):
            wide[j, d * pitch : d * pitch + 2 * HALO, :] = rows[:, j * LANES : (j + 1) * LANES]

    def pixels(c, t, j):
        return wide[j, pl.ds(c * HALO + t, dates, stride=pitch), :]

    per = SEGMENT // LANES
    segments = HALO * chunks // per
    table = jnp.concatenate(
        [
            jnp.concatenate(
                [
                    jnp.concatenate(
                        [pixels(c, *divmod(s * per + n, chunks)) for n in range(per)], axis=1
                    )
                    for c in range(2)
                ],
                axis=0,
            ).astype(BF16)
            for s in range(segments)
        ],
        axis=0,
    )

    half = SEGMENT // 2
    places = [(iota((16, LANES), 0) + 16 * n).astype(F32).astype(BF16) for n in range(half // 16)]
    one, zero = jnp.ones((16, LANES), BF16), jnp.zeros((16, LANES), BF16)

    values = []
    batch = min(BATCH, windows)
    for first in range(0, windows, batch):
        marks, highs = [], []
        for w in range(first, first + batch):
            pixel = frames[w : w + 1, :]
            low = pixel & (half - 1)
            upper = (pixel & half) == half
            keys = [jnp.where(upper, -1, low), jnp.where(upper, low, -1)]
            keys = [jnp.broadcast_to(key, (16, LANES)).astype(F32).astype(BF16) for key in keys]
            marks.append(
                jnp.concatenate(
                    [jnp.where(key == place, one, zero) for key in keys for place in places],
                    axis=0,
                )
            )
            highs.append(lax.shift_right_logical(pixel, SEGMENT.bit_length() - 1))
        high = jnp.broadcast_to(jnp.concatenate(highs, axis=1), (depth, batch * LANES))
        taken = jnp.dot(table, jnp.concatenate(marks, axis=1), preferred_element_type=F32)
        found = taken[:depth]
        for s in range(1, segments):
            found = jnp.where(high == s, taken[s * depth : (s + 1) * depth], found)
        values.extend(found[:, n * LANES : (n + 1) * LANES] for n in range(batch))
    left = []
    for w, value in enumerate(values):
        turned = jnp.concatenate([-value[dates:], value[:dates]], axis=0)
        left.append(jnp.concatenate([value[:dates], turned[:dates]], axis=1).astype(BF16))
        for n, piece in enumerate((value, turned)):
            right32[n, pl.ds(w, depth, stride=windows + 1), :] = piece
    products = lax.dot_general(
        jnp.concatenate(left, axis=0),
        jnp.concatenate(
            [
                jnp.concatenate(
                    [right32[n, at : at + windows].astype(BF16) for n in range(2)], axis=1
                )
                for at in range(0, depth * (windows + 1), windows + 1)
            ],
            axis=0,
        ),
        NT,
        preferred_element_type=F32,
    )
    owner = iota((dates, span), 1) & (windows - 1)
    cov = products[:dates]
    for w in range(1, windows):
        cov = jnp.where(owner == w, products[w * dates : (w + 1) * dates], cov)
    cov = cov * (1.0 / LOOKS)

    column = []
    for k in range(depth):
        tile, at = divmod(k * windows, LANES)
        entry = cov[:, tile * LANES : (tile + 1) * LANES]
        column.append(pltpu.roll(entry, LANES - at, 1) if at else entry)
    row = iota((dates, LANES), 0)
    power = column[0]
    for d in range(1, dates):
        power = jnp.where(row == d, column[d], power)
    inverse = lax.rsqrt(power + EPSILON)
    for k in range(depth):
        e = k % dates
        entry = (1.0 - SHRINK) * column[k] * inverse * inverse[e : e + 1]
        if k < dates:
            entry = entry + jnp.where(row == e, SHRINK, 0.0)
        gam[k] = entry

    def tree(terms):
        while len(terms) > 1:
            terms = [terms[n] + terms[n + 1] for n in range(0, len(terms), 2)]
        return terms[0]

    scale = jnp.ones((1, LANES), F32)
    real = tree([gam[e] for e in range(dates)])
    imaginary = -tree([gam[dates + e] for e in range(dates)])
    for step in range(ITERS):
        if step:
            reals = [real[e : e + 1] for e in range(dates)]
            imaginaries = [imaginary[e : e + 1] for e in range(dates)]
            real = tree(
                [gam[e] * reals[e] + gam[dates + e] * imaginaries[e] for e in range(dates)]
            )
            imaginary = tree(
                [gam[e] * imaginaries[e] - gam[dates + e] * reals[e] for e in range(dates)]
            )
        size = jnp.sum(real * real + imaginary * imaginary, axis=0, keepdims=True)
        scale = scale * lax.rsqrt(scale * scale * (size * (1.0 / dates)) + EPSILON)
    linked_real = (real * scale).astype(BF16).astype(F32)
    linked_imaginary = (imaginary * scale).astype(BF16).astype(F32)

    def over_rows(value):
        return jnp.sum(value, axis=0, keepdims=True)

    factor = 1.0 / math.sqrt(dates)
    for w in range(windows):
        t, at = (w * LOOKS) // cells, (w * LOOKS) % cells
        real = jnp.broadcast_to(linked_real[:, w : w + 1], (dates, LANES))
        imaginary = jnp.broadcast_to(linked_imaginary[:, w : w + 1], (dates, LANES))
        own_real = pixels(0, 1 + t, at // LANES)
        own_imaginary = pixels(1, 1 + t, at // LANES)
        value_real = over_rows(real * own_real + imaginary * own_imaginary) * factor
        value_imaginary = over_rows(real * own_imaginary - imaginary * own_real) * factor
        value_real = value_real.astype(BF16).astype(F32)
        value_imaginary = value_imaginary.astype(BF16).astype(F32)
        side, tile = divmod(at // LANES, chunks // 2)
        for c, value in enumerate(
            (
                value_real * real - value_imaginary * imaginary,
                value_real * imaginary + value_imaginary * real,
            )
        ):
            r = (c * LB + t) * 2 + side
            rebuilt[tile, pl.ds(r, dates, stride=4 * LB + 1), :] = value
    for d in range(dates):
        for j in range(chunks // 2):
            at = d * (4 * LB + 1)
            out[d, :, j * LANES : (j + 1) * LANES] = rebuilt[j, at : at + 4 * LB].astype(BF16)


def link(ground, frames):
    dates, _, cells = ground.shape
    windows = frames.shape[0]
    depth = 2 * dates
    vmem = pl.BlockSpec(memory_space=pltpu.VMEM)
    return pl.pallas_call(
        link_kernel,
        out_shape=jax.ShapeDtypeStruct((dates, 4 * LB, cells // 2), BF16),
        in_specs=[vmem, vmem],
        out_specs=vmem,
        scratch_shapes=[
            pltpu.VMEM((cells // LANES, dates * (2 * HALO + 1), LANES), F32),
            pltpu.VMEM((2, depth * (windows + 1), LANES), F32),
            pltpu.VMEM((depth, dates, LANES), F32),
            pltpu.VMEM((cells // (2 * LANES), dates * (4 * LB + 1), LANES), F32),
        ],
        compiler_params=grant(dates),
    )(frames, ground)


def coupling_frames(readings, native_picture_elements):
    sample_real = readings[:, 0]
    sample_imaginary = readings[:, 1]

    def pair(left, right):
        return jnp.einsum("dwm,ewm->wde", left, right, preferred_element_type=F32)

    inverse_looks = 1.0 / LOOKS
    covariance_real = (
        pair(sample_real, sample_real) + pair(sample_imaginary, sample_imaginary)
    ) * inverse_looks
    mixed = pair(sample_imaginary, sample_real)
    covariance_imaginary = (mixed - jnp.swapaxes(mixed, 1, 2)) * inverse_looks
    dates = readings.shape[0]
    inverse_root = lax.rsqrt(jnp.diagonal(covariance_real, axis1=1, axis2=2) + EPSILON)
    outer = inverse_root[:, :, None] * inverse_root[:, None, :]
    identity = jnp.eye(dates, dtype=F32)
    coherence_real = (1.0 - SHRINK) * covariance_real * outer + SHRINK * identity
    coherence_imaginary = (1.0 - SHRINK) * covariance_imaginary * outer
    vector_real = jnp.ones(inverse_root.shape, F32)
    vector_imaginary = jnp.zeros(inverse_root.shape, F32)

    def apply_matrix(matrix, vector):
        return jnp.einsum("wde,we->wd", matrix, vector, precision=lax.Precision.HIGHEST)

    for iteration in range(ITERS):
        image_real = apply_matrix(coherence_real, vector_real) - apply_matrix(
            coherence_imaginary, vector_imaginary
        )
        image_imaginary = apply_matrix(coherence_real, vector_imaginary) + apply_matrix(
            coherence_imaginary, vector_real
        )
        power = image_real * image_real + image_imaginary * image_imaginary
        factor = lax.rsqrt(jnp.mean(power, axis=1, keepdims=True) + EPSILON)
        vector_real = image_real * factor
        vector_imaginary = image_imaginary * factor
    coupled_result = jnp.stack([vector_real, vector_imaginary]).astype(BF16)

    def project(history, pixels):
        return jnp.einsum("wd,dwm->wm", history, pixels, preferred_element_type=F32)

    scaling = 1.0 / math.sqrt(dates)
    own_real = native_picture_elements[:, 0]
    own_imaginary = native_picture_elements[:, 1]
    compressed_real = (
        project(coupled_result[0], own_real) + project(coupled_result[1], own_imaginary)
    ) * scaling
    compressed_imaginary = (
        project(coupled_result[0], own_imaginary) - project(coupled_result[1], own_real)
    ) * scaling
    condensed_result = jnp.stack([compressed_real, compressed_imaginary]).astype(BF16)
    return (condensed_result, coupled_result)


def link_plain(ground, frames):
    dates, _, cells = ground.shape
    windows = frames.shape[0]
    extended = ground.reshape(dates, 2, HALO, cells)
    flat = extended.reshape(dates, 2, HALO * cells)
    readings = jnp.take(flat, frames.reshape(-1), axis=2).reshape(dates, 2, windows, LOOKS)
    native = extended[:, :, 1 : LB + 1].reshape(dates, 2, windows, LOOKS)
    condensed_result, coupled_result = coupling_frames(readings, native)
    history_real = coupled_result[0].astype(F32).T[:, :, None]
    history_imaginary = coupled_result[1].astype(F32).T[:, :, None]
    value_real = condensed_result[0].astype(F32)[None]
    value_imaginary = condensed_result[1].astype(F32)[None]
    rebuilt = jnp.stack(
        [
            value_real * history_real - value_imaginary * history_imaginary,
            value_real * history_imaginary + value_imaginary * history_real,
        ],
        axis=1,
    ).astype(BF16)
    return rebuilt.reshape(dates, 4 * LB, cells // 2)


def dft_tables(length, span):
    first, second = np.arange(span)[:, None], np.arange(span)[None, :]
    angle = (first % length) * (second % length) % length * (2.0 * math.pi / length)
    inside = first // length == second // length
    return np.where(inside, np.cos(angle), 0.0), np.where(inside, np.sin(angle), 0.0)


def patch_kernel(range_table, ahead_table, back_table, mine, out, wide):
    blocks, rows, _ = mine.shape
    cells = out.shape[3]
    chunks = cells // LANES

    def cut(value, j):
        return value[:, j * LANES : (j + 1) * LANES]

    for b in range(blocks):
        block = mine[b].astype(F32)
        for j in range(chunks // 2):
            wide[j, b * (rows + 1) : b * (rows + 1) + rows, :] = cut(block, j)

    def lines_of(c, j):
        side, j = divmod(j, chunks // 2)
        pieces = [
            wide[j, pl.ds((c * LB + t) * 2 + side, blocks, stride=rows + 1), :] for t in range(LB)
        ]
        return jnp.concatenate(pieces, axis=0).astype(BF16)

    first = jnp.concatenate(
        [
            jnp.concatenate([lines_of(0, j), lines_of(1, j)], axis=1)
            for j in range(chunks)
        ],
        axis=0,
    )

    def by_chunk(real, imaginary):
        return jnp.concatenate(
            [
                jnp.concatenate([cut(real, j), cut(imaginary, j)], axis=1)
                for j in range(chunks)
            ],
            axis=0,
        )

    def by_line(value, c):
        return jnp.concatenate(
            [cut(value[j * PATCH : (j + 1) * PATCH], c) for j in range(chunks)], axis=1
        )

    table = range_table[...]
    across = jnp.dot(first, table, preferred_element_type=F32).astype(BF16)
    across = jnp.concatenate([by_line(across, 0), by_line(across, 1)], axis=0)
    spectrum = jnp.dot(ahead_table[...], across, preferred_element_type=F32)
    real, imaginary = spectrum[:PATCH], spectrum[PATCH:]
    power = real * real + imaginary * imaginary
    total = jnp.sum(power, axis=0, keepdims=True)
    total = jnp.concatenate([cut(total, j) for j in range(chunks)], axis=0)
    pieces = []
    for _ in range(3):
        pieces.append(total.astype(BF16))
        total = total - pieces[-1].astype(F32)
    bits = PATCH.bit_length() - 1
    first, second = iota((LANES, LANES), 0), iota((LANES, LANES), 1)
    ones = lax.shift_right_logical(first, bits) == lax.shift_right_logical(second, bits)
    ones = jnp.where(ones, 1.0, 0.0).astype(BF16)
    pieces = jnp.concatenate(pieces, axis=0)
    pieces = jnp.dot(pieces, ones, preferred_element_type=F32)
    total = pieces[:chunks] + (pieces[chunks : 2 * chunks] + pieces[2 * chunks :])
    mean = total * (1.0 / (PATCH * PATCH)) + EPSILON
    level = jnp.sqrt(lax.rsqrt(mean))
    level = jnp.concatenate([level[j : j + 1] for j in range(chunks)], axis=1)
    ramp = lax.rsqrt(lax.rsqrt(jnp.maximum(power, SMALLEST)))
    weighted = jnp.concatenate([real * ramp * level, imaginary * ramp * level], axis=0)
    weighted = weighted.astype(BF16)
    back = jnp.dot(back_table[...], weighted, preferred_element_type=F32).astype(BF16)
    back = by_chunk(back[:PATCH], back[PATCH:])
    final = lax.dot_general(back, table, NT, preferred_element_type=F32)
    final = (final * (1.0 / (PATCH * PATCH))).astype(BF16)
    for c in range(2):
        out[0, c] = by_line(final, c)


def patch_filter(mine, lines):
    cells = 2 * mine.shape[2]
    blocks = PATCH // LB
    cosine, sine = dft_tables(PATCH, LANES)
    range_table = np.block([[cosine, -sine], [sine, cosine]])
    cosine, sine = dft_tables(PATCH, PATCH)
    order = np.arange(PATCH).reshape(blocks, LB).T.reshape(-1)
    ahead = np.block([[cosine[:, order], sine[:, order]], [-sine[:, order], cosine[:, order]]])
    back = np.block([[cosine, -sine], [sine, cosine]])
    tables = [jnp.asarray(entry, F32).astype(BF16) for entry in (range_table, ahead, back)]
    return pl.pallas_call(
        patch_kernel,
        grid=(lines // PATCH,),
        out_shape=jax.ShapeDtypeStruct((1, 2, lines, cells), BF16),
        in_specs=[
            pl.BlockSpec((2 * LANES, 2 * LANES), lambda p: (0, 0)),
            pl.BlockSpec((2 * PATCH, 2 * PATCH), lambda p: (0, 0)),
            pl.BlockSpec((2 * PATCH, 2 * PATCH), lambda p: (0, 0)),
            pl.BlockSpec((blocks, *mine.shape[1:]), lambda p: (p, 0, 0)),
        ],
        out_specs=pl.BlockSpec((1, 2, PATCH, cells), lambda p: (0, 0, p, 0)),
        scratch_shapes=[pltpu.VMEM((cells // (2 * LANES), blocks * (4 * LB + 1), LANES), F32)],
        compiler_params=grant(lines // LB),
    )(*tables, mine)


def on_device(
    salvo_records, stencil_weights, zone_drifts, seam_sweeps, prior_sweeps, viewing_frames
):
    devices = lax.axis_size("date")
    merged = seam(
        salvo_records, stencil_weights, zone_drifts, seam_sweeps, prior_sweeps, devices
    )
    ground = lax.all_to_all(merged, "date", split_axis=0, concat_axis=0, tiled=True)
    windows = viewing_frames.shape[0]
    fits = devices <= 32 and devices % 16 == 0 and windows % 2 == 0 and LANES % windows == 0
    fits = fits and salvo_records.shape[4] % SEGMENT == 0
    rebuilt = (link if fits else link_plain)(ground, viewing_frames)
    mine = lax.all_to_all(rebuilt, "date", split_axis=0, concat_axis=0, tiled=True)
    return patch_filter(mine, LB * devices)


def solution(mesh):
    in_specs = (
        P(("group", "date"), None, None, None, None),
        P(("group", "date"), None, None),
        P(("group", "date"), None),
        P(("group", "date"), None),
        P(("group", "date")),
        P(("group", "date"), None),
    )
    out_specs = P(("group", "date"), None, None, None)
    return jax.shard_map(
        on_device, mesh=mesh, in_specs=in_specs, out_specs=out_specs, check_vma=False
    )
```
